32 devices in a mesh: band: 4 (over y, core), aperture: 8 (over z, x).
Axes of the slice: x: 2, y: 2, z: 4, core: 2. Of those that a mesh axis runs over, the one named last changes fastest.
Arguments:
- raw_echoes: bfloat16 [1024, 2, 4096], P('aperture', None, 'band'), may hold values from -6 to 6
- pulse_order: int32 [8, 4, 32], P('aperture', 'band'), may hold values from 0 to 31, each once within a row
- matched: float32 [2, 4096], replicated, may hold values from -6 to 6
- offsets: int32 [10, 2, 2, 1], replicated, may hold values from 0 to 16
- fraction: float32 [10, 2, 2], replicated, may hold values from 0 to 0.4
- tilt_angle: float32 [10, 2], replicated, may hold values from -3.140625 to 3.140625
Outputs:
- speckle_image: float32 [1024, 128], P(('band', 'aperture'))
The draws below stay inside these ranges and needn't reach their ends.
Inputs may be any that keep to these rules, and one draw needn't show every extreme that they name: `pulse_order`: each row of 32 entries names every number below 32 once.
All inputs are finite; a program needn't handle non-finite values.
Results may differ from the reference program's by a relative error of at most 0.0025.
Values may be sent and summed in bfloat16 or wider, within the bound.
No kernel may reach another device: no remote copies, remote signals or barrier semaphores. Data moves between devices by JAX's collectives and lax.ppermute only.
A program may use at most 64 MiB of HBM per device.

```python
import math
import jax
import jax.numpy as jnp
from jax import lax

FREQ = 4096
R = 128
LOCAL_LEV = 5
SHIFT = 8
PUL_DEV = 32
NBD = 4
NAP = 8
LEVELS = 10
PULSES = 1024
RBLK = 1
N_BAND = 4
N_APERTURE = 8


def touch_ends(values, own_key, least, top_value):
    spot = [jax.random.randint(jax.random.fold_in(own_key, axis), (), 0, length) for axis, length in enumerate(values.shape)]
    longest = values.shape.index(max(values.shape))
    next_to = spot[:longest] + [(spot[longest] + 1) % values.shape[longest]] + spot[longest + 1:]
    return values.at[tuple(spot)].set(least).at[tuple(next_to)].set(top_value)


def steps_of(stream_key, extent, split, low, high):
    def one(axis_at, shards_of):
        steps = jax.random.uniform(jax.random.fold_in(jax.random.fold_in(stream_key, 6), axis_at), (shards_of,), jnp.float32, low / len(split), high / len(split))
        return jnp.repeat(jnp.exp(steps), extent[axis_at] // shards_of).reshape((-1,) + (1,) * (len(extent) - axis_at - 1))

    level = one(*split[0])
    for cut in split[1:]:
        level = level * one(*cut)
    return level


def normal_values(key, extent, scale, limit, pieces=(), kind=jnp.bfloat16):
    result = scale * jax.random.normal(key, extent, jnp.float32)
    if pieces:
        result = result * steps_of(key, extent, pieces, -0.22, 0.18)
    return jnp.clip(result, -limit, limit).astype(kind)


def setup_inputs(seed: int = 0) -> dict:
    streams_of = jax.random.split(jax.random.key(seed), 7)
    raw_echoes = normal_values(streams_of[0], (PULSES, 2, FREQ), 1.0, 6.0, ((0, 8), (2, 4)))
    pulse_order = jax.vmap(lambda own: jax.random.permutation(own, PUL_DEV))(jax.random.split(streams_of[1], NAP * NBD)).reshape((NAP, NBD, PUL_DEV)).astype(jnp.int32)
    matched = normal_values(streams_of[2], (2, FREQ), 1.0, 6.0, (), jnp.float32)
    offsets = touch_ends(jax.random.randint(streams_of[3], (LEVELS, 2, 2, RBLK), 0, 2 * SHIFT + 1), jax.random.fold_in(streams_of[3], 1), 0, 2 * SHIFT).astype(jnp.int32)
    fraction = jnp.clip(jax.random.uniform(streams_of[4], (LEVELS, 2, 2), jnp.float32, 0.0, 0.4), 0.0, 0.4)
    tilt_angle = jnp.clip(jax.random.uniform(streams_of[5], (LEVELS, 2), jnp.float32, -3.140625, 3.140625), -3.140625, 3.140625)
    return {"raw_echoes": raw_echoes, "pulse_order": pulse_order, "matched": matched, "offsets": offsets, "fraction": fraction, "tilt_angle": tilt_angle}


HIGHEST = lax.Precision.HIGHEST

def range_table(matched_part, freq_start, bin_start, bin_count):
    freq_count = matched_part.shape[1]
    freq_index = freq_start + jnp.arange(freq_count, dtype=jnp.int32)
    bin_index = bin_start + jnp.arange(bin_count, dtype=jnp.int32)
    phase_turns = freq_index[:, None] * bin_index[None, :] % FREQ
    phase_angle = phase_turns.astype(jnp.float32) * (2.0 * math.pi / FREQ)
    cosine = jnp.cos(phase_angle)
    sine_part = jnp.sin(phase_angle)
    spec_real = matched_part[0][:, None]
    spec_imag = matched_part[1][:, None]
    norm_scale = 1.0 / math.sqrt(FREQ)
    table_real = (spec_real * cosine - spec_imag * sine_part) * norm_scale
    table_imag = (spec_real * sine_part + spec_imag * cosine) * norm_scale
    upper_rows = jnp.concatenate([table_real, table_imag], axis=1)
    lower_rows = jnp.concatenate([-table_imag, table_real], axis=1)
    return jnp.concatenate([upper_rows, lower_rows], axis=0).astype(jnp.bfloat16)

def interp_kernel(shift_frac):
    in_pos = jnp.arange(128, dtype=jnp.float32)[:, None]
    out_pos = jnp.arange(128, dtype=jnp.float32)[None, :]
    distance = in_pos - out_pos - shift_frac
    tapered = jnp.sinc(distance) * jnp.exp(-(distance / 2.5) ** 2)
    return jnp.where(jnp.abs(distance) <= 4.0, tapered, jnp.zeros_like(tapered))

def merge_pair(first_child, second_child, tree_level, beam_start, offsets, fraction, tilt_angle):
    sub_count = first_child.shape[0]
    row_count = first_child.shape[1]
    range_width = first_child.shape[3]
    block_count = range_width // 128
    halves = []
    for parity in range(2):
        beam_index = (beam_start + 2 * jnp.arange(row_count, dtype=jnp.int32) + parity).astype(jnp.float32)
        position = 2.0 * (beam_index + 0.5) / 2.0 ** (tree_level + 1) - 1.0
        summed = jnp.zeros(first_child.shape, jnp.float32)
        for child_index, child_image in enumerate((first_child, second_child)):
            padded = jnp.pad(child_image, ((0, 0), (0, 0), (0, 0), (SHIFT, SHIFT)))
            windows = []
            for block_index in range(block_count):
                start_cell = (block_index * 128 + offsets[tree_level, child_index, parity, block_index]).astype(jnp.int32)
                windows.append(lax.dynamic_slice_in_dim(padded, start_cell, 128, 3))
            stacked = jnp.stack(windows, axis=3)
            kernel = interp_kernel(fraction[tree_level, child_index, parity])
            shifted = jnp.einsum('nrckw,wo->nrcko', stacked, kernel, precision=HIGHEST)
            shifted = shifted.reshape(first_child.shape)
            phase_angle = tilt_angle[tree_level, child_index] * position
            cosine = jnp.cos(phase_angle)[None, :, None]
            sine_part = jnp.sin(phase_angle)[None, :, None]
            real_part = shifted[:, :, 0]
            imag_part = shifted[:, :, 1]
            summed = summed + jnp.stack([real_part * cosine - imag_part * sine_part, real_part * sine_part + imag_part * cosine], axis=2)
        halves.append(summed * (1.0 / math.sqrt(2.0)))
    parent = jnp.stack(halves, axis=2)
    return parent.reshape(sub_count, 2 * row_count, 2, range_width)

def box_sum(values):
    row_count = values.shape[1]
    range_width = values.shape[2]
    padded = jnp.pad(values, ((0, 0), (2, 2), (2, 2)))
    across = padded[:, 0:row_count, :]
    for offset_row in range(1, 5):
        across = across + padded[:, offset_row:offset_row + row_count, :]
    summed = across[:, :, 0:range_width]
    for offset_col in range(1, 5):
        summed = summed + across[:, :, offset_col:offset_col + range_width]
    return summed

def speckle(intensity):
    cell_count = box_sum(jnp.ones(intensity.shape, jnp.float32))
    local_mean = box_sum(intensity) / cell_count
    local_square = box_sum(intensity * intensity) / cell_count
    lee_gain = (local_square - local_mean * local_mean) / (local_square - 0.75 * local_mean * local_mean + 0.001)
    return local_mean + lee_gain * (intensity - local_mean)

def reference(raw_echoes, pulse_order, matched, offsets, fraction, tilt_angle):
    group_count = N_BAND * N_APERTURE
    pulse_rows = (jnp.arange(group_count, dtype=jnp.int32)[:, None] * PUL_DEV + pulse_order.reshape(group_count, PUL_DEV).astype(jnp.int32)).reshape(-1)
    echoes = raw_echoes[pulse_rows].reshape(group_count, PUL_DEV, 2 * FREQ)
    dft_table = range_table(matched, 0, 0, R).astype(jnp.float32)

    def compress(group_echoes):
        return jnp.dot(group_echoes.astype(jnp.float32), dft_table, precision=HIGHEST)
    profiles = lax.map(compress, echoes)
    images = profiles.reshape(PULSES, 1, 2, R)
    for tree_level in range(LEVELS):
        images = merge_pair(images[0::2], images[1::2], tree_level, 0, offsets, fraction, tilt_angle)
    final_image = images[0]
    intensity = final_image[:, 0] ** 2 + final_image[:, 1] ** 2
    filtered = speckle(intensity.reshape(group_count, PUL_DEV, R))
    tile_index = jnp.arange(group_count, dtype=jnp.int32)
    source = tile_index % N_APERTURE * N_BAND + tile_index // N_APERTURE
    cross_bits = LEVELS - LOCAL_LEV
    reversed_index = jnp.zeros_like(source)
    for bit_index in range(cross_bits):
        reversed_index = reversed_index + source // 2 ** bit_index % 2 * 2 ** (cross_bits - 1 - bit_index)
    return filtered[reversed_index].reshape(PULSES, R)
```

```python
import functools
import math

import jax
import jax.numpy as jnp
from jax import lax
from jax.experimental import pallas as pl
from jax.experimental.pallas import tpu as pltpu
from jax.sharding import PartitionSpec as P

R = 128
SHIFT = 8
LANES = 128
VMEM = pltpu.VMEM
SMEM = pltpu.SMEM


def iota(shape, axis):
    return lax.broadcasted_iota(jnp.int32, shape, axis)


def bit_reversed(value, bits):
    result = value & 0
    for bit in range(bits):
        result = result | (((value >> bit) & 1) << (bits - 1 - bit))
    return result


def halves_of(value):
    high = value.astype(jnp.bfloat16)
    low = (value - high.astype(jnp.float32)).astype(jnp.bfloat16)
    return high, low


def compress_kernel(total_freq, echo_ref, matched_ref, prof_ref, table_ref):
    pulses = echo_ref.shape[0]
    freq = table_ref.shape[1]
    start = lax.axis_index("band") * freq
    scale = 1.0 / math.sqrt(total_freq)
    turn = 2.0 * math.pi / total_freq
    for chunk in range(freq // LANES):
        first = start + chunk * LANES
        lanes = pl.ds(pl.multiple_of(first, LANES), LANES)
        f_index = first + iota((8, LANES), 1)
        angle = ((f_index * iota((8, LANES), 0)) % total_freq).astype(jnp.float32) * turn
        cos_a, sin_a = jnp.cos(angle), jnp.sin(angle)
        angle = ((f_index * 8) % total_freq).astype(jnp.float32) * turn
        cos_w, sin_w = jnp.cos(angle), jnp.sin(angle)
        spec_r = matched_ref[0:1, lanes] * scale
        spec_i = matched_ref[1:2, lanes] * scale
        low_r = spec_r * cos_a - spec_i * sin_a
        low_i = spec_r * sin_a + spec_i * cos_a
        re = jnp.concatenate([low_r, low_r * cos_w - low_i * sin_w], axis=0)
        im = jnp.concatenate([low_i, low_r * sin_w + low_i * cos_w], axis=0)
        two_r = cos_w * cos_w - sin_w * sin_w
        two_i = 2.0 * cos_w * sin_w
        two_r = jnp.concatenate([two_r, two_r], axis=0)
        two_i = jnp.concatenate([two_i, two_i], axis=0)
        here = pl.ds(chunk * LANES, LANES)
        for block in range(R // 16):
            table_ref[pl.ds(block * 16, 16), here] = re.astype(jnp.bfloat16)
            table_ref[pl.ds(R + block * 16, 16), here] = im.astype(jnp.bfloat16)
            if block + 1 < R // 16:
                re, im = re * two_r - im * two_i, re * two_i + im * two_r
    table = table_ref[...]
    dims = (((1,), (1,)), ((), ()))
    from_re = lax.dot_general(
        echo_ref[:, 0:freq], table, dims, preferred_element_type=jnp.float32
    )
    from_im = lax.dot_general(
        echo_ref[:, freq : 2 * freq], table, dims, preferred_element_type=jnp.float32
    )
    prof_ref[0:pulses, :] = from_re[:, 0:R] - from_im[:, R:]
    prof_ref[pulses:, :] = from_re[:, R:] + from_im[:, 0:R]


def build_matrices(first_level, count, offsets_ref, fraction_ref, high_ref, low_ref):
    lane = iota((8, LANES), 1)
    tap = jnp.where(lane < LANES // 2, -lane, LANES - lane).astype(jnp.float32)
    row = iota((8, LANES), 0)
    entries = 4 * count
    base = 4 * first_level
    in_bin, out_bin = iota((R, R), 0), iota((R, R), 1)
    for block in range((entries + 7) // 8):
        shift = jnp.zeros((8, LANES), jnp.float32)
        for sub in range(min(8, entries - block * 8)):
            shift = jnp.where(row == sub, fraction_ref[base + block * 8 + sub], shift)
        dist = tap - shift
        turn = math.pi * dist
        near = jnp.abs(dist) < 1e-12
        sinc = jnp.where(near, 1.0, jnp.sin(turn) / jnp.where(near, 1.0, turn))
        taper = sinc * jnp.exp(-((dist / 2.5) ** 2))
        taper = jnp.where(jnp.abs(dist) <= 4.0, taper, 0.0)
        for sub in range(min(8, entries - block * 8)):
            entry = block * 8 + sub
            moved = offsets_ref[base + entry] - SHIFT
            one = jnp.broadcast_to(taper[sub : sub + 1, :], (8, LANES))
            one = pltpu.roll(one, (LANES - moved) % LANES, 1)
            wide = jnp.broadcast_to(one[0:1, :], (R, LANES))
            wide = pltpu.roll(wide, 0, 1, stride=1, stride_axis=0)
            window = in_bin - moved
            keep = (window >= 0) & (window < R) & (jnp.abs(window - out_bin) <= 4)
            high, low = halves_of(jnp.where(keep, wide, 0.0))
            at = (entry // 2, slice(None), pl.ds((entry % 2) * LANES, LANES))
            high_ref[at] = high
            low_ref[at] = low


def phase_tables(first_level, count, half, inner_bits, tile, tilt_ref):
    bits = half.bit_length() - 1
    lane = iota((1, LANES), 1)
    angle = jnp.zeros((1, LANES), jnp.float32)
    step = jnp.ones((1, LANES), jnp.float32)
    mask = jnp.zeros((1, LANES), jnp.int32)
    tile_start = jnp.zeros((1, LANES), jnp.int32)
    for level in range(count):
        width = inner_bits + level
        here = (lane >> 2) == level
        step = jnp.where(here, 2.0 ** -(first_level + level), step)
        mask = jnp.where(here, 2**width - 1, mask)
        tile_start = jnp.where(here, tile * 2**width, tile_start)
        for child in range(2):
            angle = jnp.where(
                (lane >> 1) == 2 * level + child,
                tilt_ref[2 * (first_level + level) + child],
                angle,
            )
    order = bit_reversed(iota((half, LANES), 0), bits)
    beam = tile_start + (order & mask)
    j_index = (2 * beam + (lane & 1)).astype(jnp.float32)
    phi = angle * ((j_index + 0.5) * step - 1.0)
    norm = 1.0 / math.sqrt(2.0)
    return jnp.cos(phi) * norm, jnp.sin(phi) * norm


def level_step(level, half, source, cos_t, sin_t, high_ref, low_ref):
    products = []
    for child in range(2):
        held = source[pl.ds(child, 2 * half, stride=2), :]
        high, low = halves_of(held)
        m_high, m_low = high_ref[2 * level + child], low_ref[2 * level + child]
        dot = functools.partial(jnp.dot, preferred_element_type=jnp.float32)
        products.append(dot(high, m_high) + (dot(low, m_high) + dot(high, m_low)))
    result = []
    for parity in range(2):
        re = im = None
        for child in range(2):
            entry = 4 * level + 2 * child + parity
            co = cos_t[:, entry : entry + 1]
            si = sin_t[:, entry : entry + 1]
            p_re = products[child][0:half, parity * R : (parity + 1) * R]
            p_im = products[child][half:, parity * R : (parity + 1) * R]
            r_new = p_re * co - p_im * si
            i_new = p_re * si + p_im * co
            re = r_new if re is None else re + r_new
            im = i_new if im is None else im + i_new
        result.append((re, im))
    return result


def local_kernel(count, devices, *refs):
    bands = lax.axis_size("band")
    orders = refs[:bands]
    prof_ref, offsets_ref, fraction_ref, tilt_ref = refs[bands : bands + 4]
    out_ref, high_ref, low_ref, image_ref = refs[bands + 4 :]
    pulses = prof_ref.shape[0] // 2
    half = pulses // 2
    group = pulses // bands
    build_matrices(0, count, offsets_ref, fraction_ref, high_ref, low_ref)
    cos_t, sin_t = phase_tables(0, count, half, 0, 0, tilt_ref)
    me = lax.axis_index("band")
    for apart in range(bands):
        start = pl.multiple_of((me ^ apart) * group, group)
        for pulse in range(group):
            row = start + orders[apart][pulse]
            for part in range(0, 2 * pulses, pulses):
                value = prof_ref[pl.ds(part + row, 1), :]
                image_ref[0, pl.ds(part + start + pulse, 1), :] = value
    kept = pulses // devices
    for level in range(count):
        source, target = image_ref.at[level % 2], image_ref.at[(level + 1) % 2]
        result = level_step(level, half, source, cos_t, sin_t, high_ref, low_ref)
        for parity in range(2):
            for part in range(2):
                value = result[parity][part]
                if level + 1 < count:
                    target[pl.ds(part * pulses + parity * half, half), :] = value
                    continue
                size = min(half, devices)
                for piece in range(half // size):
                    row = parity * half + piece * size
                    begin = (row % devices) * 2 * kept + part * kept + row // devices
                    out_ref[pl.ds(begin, size, stride=2 * kept), :] = value[
                        piece * size : (piece + 1) * size
                    ]


def box(rows):
    total = rows[0]
    for row in rows[1:]:
        total = total + row
    lane = iota(total.shape, 1)
    summed = total
    for off in (1, 2):
        right = pltpu.roll(total, off, 1)
        left = pltpu.roll(total, LANES - off, 1)
        summed = summed + jnp.where(lane >= off, right, 0.0)
        summed = summed + jnp.where(lane < LANES - off, left, 0.0)
    return summed


def near_count(position, size):
    return jnp.minimum(position, 2) + jnp.minimum(size - 1 - position, 2) + 1


def final_kernel(first_level, count, recv_ref, offsets_ref, fraction_ref, tilt_ref, out_ref,
                 high_ref, low_ref, image_ref, pad_ref):
    bands, apertures = lax.axis_size("band"), lax.axis_size("aperture")
    devices = bands * apertures
    rows = out_ref.shape[0]
    half = rows // 2
    kept = rows // apertures
    tile_bits = devices.bit_length() - 1
    inner = kept.bit_length() - 1
    build_matrices(first_level, count, offsets_ref, fraction_ref, high_ref, low_ref)
    place = lax.axis_index("aperture") * bands + lax.axis_index("band")
    tile = bit_reversed(place, tile_bits)
    cos_t, sin_t = phase_tables(first_level, count, half, inner, tile, tilt_ref)
    for part in range(2):
        for beam in range(kept):
            total = None
            for band in range(bands):
                begin = band * 2 * kept + part * kept + beam
                value = recv_ref[pl.ds(begin, apertures, stride=bands * 2 * kept), :]
                total = value if total is None else total + value
            image_ref[0, pl.ds(part * rows + beam * apertures, apertures), :] = total
    for level in range(count):
        source, target = image_ref.at[level % 2], image_ref.at[(level + 1) % 2]
        result = level_step(level, half, source, cos_t, sin_t, high_ref, low_ref)
        for parity in range(2):
            for part in range(2):
                target[pl.ds(part * rows + parity * half, half), :] = result[parity][part]
    last = image_ref.at[count % 2]
    power = last[0:rows, :] ** 2 + last[rows : 2 * rows, :] ** 2
    image_ref[(count + 1) % 2, 0:rows, :] = power
    edge = 8
    for part in range(2):
        pad_ref[part, 0:edge, :] = jnp.zeros((edge, LANES), jnp.float32)
        pad_ref[part, edge + rows :, :] = jnp.zeros((edge, LANES), jnp.float32)
    bits = rows.bit_length() - 1
    for row in range(rows):
        from_row = bit_reversed(row, bits)
        pad_ref[0, edge + row : edge + row + 1, :] = image_ref[
            (count + 1) % 2, from_row : from_row + 1, :
        ]
    power = pad_ref[0, edge : edge + rows, :]
    pad_ref[1, edge : edge + rows, :] = power * power
    sums = [
        box([pad_ref[part, edge + off : edge + off + rows, :] for off in range(-2, 3)])
        for part in range(2)
    ]
    shape = (rows, LANES)
    cells = near_count(iota(shape, 0), rows) * near_count(iota(shape, 1), LANES)
    cells = cells.astype(jnp.float32)
    mean, square = sums[0] / cells, sums[1] / cells
    gain = (square - mean * mean) / (square - 0.75 * mean * mean + 0.001)
    out_ref[...] = mean + gain * (power - mean)


def body(raw_echoes, pulse_order, matched, offsets, fraction, tilt_angle):
    bands, apertures = lax.axis_size("band"), lax.axis_size("aperture")
    devices = bands * apertures
    pulses, _, freq = raw_echoes.shape
    group = pulse_order.shape[-1]
    levels = tilt_angle.shape[0]
    local = pulses.bit_length() - 1
    order = pulse_order.reshape(group)
    orders = [order]
    for apart in range(1, bands):
        orders.append(lax.ppermute(order, "band", [(n, n ^ apart) for n in range(bands)]))
    offsets, fraction = offsets.reshape(-1), fraction.reshape(-1)
    tilt = tilt_angle.reshape(-1)
    vmem, smem = pl.BlockSpec(memory_space=VMEM), pl.BlockSpec(memory_space=SMEM)
    profiles = pl.pallas_call(
        functools.partial(compress_kernel, matched.shape[1]),
        out_shape=jax.ShapeDtypeStruct((2 * pulses, R), jnp.float32),
        in_specs=[vmem, vmem],
        out_specs=vmem,
        scratch_shapes=[VMEM((2 * R, freq), jnp.bfloat16)],
        cost_estimate=pl.CostEstimate(
            flops=8 * pulses * freq * R, bytes_accessed=4 * pulses * freq, transcendentals=0
        ),
        name="compress",
    )(raw_echoes.reshape(pulses, 2 * freq), matched)
    kept = pulses // devices
    sent = pl.pallas_call(
        functools.partial(local_kernel, local, devices),
        out_shape=jax.ShapeDtypeStruct((devices * 2 * kept, R), jnp.float32),
        in_specs=[smem] * bands + [vmem, smem, smem, smem],
        out_specs=vmem,
        scratch_shapes=[
            VMEM((2 * local, R, 2 * R), jnp.bfloat16),
            VMEM((2 * local, R, 2 * R), jnp.bfloat16),
            VMEM((2, 2 * pulses, R), jnp.float32),
        ],
        name="levels",
    )(*orders, profiles, offsets, fraction, tilt)
    received = lax.all_to_all(
        sent.reshape(devices, 2 * kept, R), ("aperture", "band"), 0, 0, tiled=True
    ).reshape(devices * 2 * kept, R)
    rows = kept * apertures
    rest = levels - local
    return pl.pallas_call(
        functools.partial(final_kernel, local, rest),
        out_shape=jax.ShapeDtypeStruct((rows, R), jnp.float32),
        in_specs=[vmem, smem, smem, smem],
        out_specs=vmem,
        scratch_shapes=[
            VMEM((2 * rest, R, 2 * R), jnp.bfloat16),
            VMEM((2 * rest, R, 2 * R), jnp.bfloat16),
            VMEM((2, 2 * rows, R), jnp.float32),
            VMEM((2, rows + 16, R), jnp.float32),
        ],
        name="finish",
    )(received, offsets, fraction, tilt)


def solution(mesh):
    in_specs = (P("aperture", None, "band"), P("aperture", "band", None), P(), P(), P(), P())
    out_specs = P(("band", "aperture"), None)
    return jax.shard_map(body, mesh=mesh, in_specs=in_specs, out_specs=out_specs, check_vma=False)
```

```python
import functools
import math

import jax
import jax.numpy as jnp
from jax import lax
from jax.experimental import pallas as pl
from jax.experimental.pallas import tpu as pltpu
from jax.sharding import PartitionSpec as P

R = 128
SHIFT = 8
LANES = 128
VMEM = pltpu.VMEM
SMEM = pltpu.SMEM


def iota(shape, axis):
    return lax.broadcasted_iota(jnp.int32, shape, axis)


def bit_reversed(value, bits):
    result = value & 0
    for bit in range(bits):
        result = result | (((value >> bit) & 1) << (bits - 1 - bit))
    return result


def halves_of(value):
    high = value.astype(jnp.bfloat16)
    low = (value - high.astype(jnp.float32)).astype(jnp.bfloat16)
    return high, low


def make_table(total_freq, start, matched_ref, table_ref):
    freq = table_ref.shape[1]
    scale = 1.0 / math.sqrt(total_freq)
    turn = 2.0 * math.pi / total_freq
    for chunk in range(freq // LANES):
        first = start + chunk * LANES
        lanes = pl.ds(pl.multiple_of(first, LANES), LANES)
        f_index = first + iota((8, LANES), 1)
        angle = ((f_index * iota((8, LANES), 0)) % total_freq).astype(jnp.float32) * turn
        cos_a, sin_a = jnp.cos(angle), jnp.sin(angle)
        angle = ((f_index * 8) % total_freq).astype(jnp.float32) * turn
        cos_w, sin_w = jnp.cos(angle), jnp.sin(angle)
        spec_r = matched_ref[0:1, lanes] * scale
        spec_i = matched_ref[1:2, lanes] * scale
        low_r = spec_r * cos_a - spec_i * sin_a
        low_i = spec_r * sin_a + spec_i * cos_a
        re = jnp.concatenate([low_r, low_r * cos_w - low_i * sin_w], axis=0)
        im = jnp.concatenate([low_i, low_r * sin_w + low_i * cos_w], axis=0)
        two_r = cos_w * cos_w - sin_w * sin_w
        two_i = 2.0 * cos_w * sin_w
        two_r = jnp.concatenate([two_r, two_r], axis=0)
        two_i = jnp.concatenate([two_i, two_i], axis=0)
        here = pl.ds(chunk * LANES, LANES)
        for block in range(R // 16):
            table_ref[pl.ds(block * 16, 16), here] = re.astype(jnp.bfloat16)
            table_ref[pl.ds(R + block * 16, 16), here] = im.astype(jnp.bfloat16)
            if block + 1 < R // 16:
                re, im = re * two_r - im * two_i, re * two_i + im * two_r


def build_matrices(levels, offsets_ref, fraction_ref, high_ref, low_ref):
    lane = iota((8, LANES), 1)
    tap = jnp.where(lane < LANES // 2, -lane, LANES - lane).astype(jnp.float32)
    row = iota((8, LANES), 0)
    entries = [(n, c, p) for n in range(levels) for c in range(2) for p in range(2)]
    edge = 2 * SHIFT
    out_bin, in_bin = iota((edge, R), 1), iota((edge, R), 0)
    for block in range(0, len(entries), 8):
        here = entries[block : block + 8]
        shift = jnp.zeros((8, LANES), jnp.float32)
        for sub, (level, child, parity) in enumerate(here):
            shift = jnp.where(row == sub, fraction_ref[child, parity, level], shift)
        dist = tap - shift
        turn = math.pi * dist
        near = jnp.abs(dist) < 1e-12
        sinc = jnp.where(near, 1.0, jnp.sin(turn) / jnp.where(near, 1.0, turn))
        taper = sinc * jnp.exp(-((dist / 2.5) ** 2))
        taper = jnp.where(jnp.abs(dist) <= 4.0, taper, 0.0)
        for sub, (level, child, parity) in enumerate(here):
            moved = offsets_ref[child, parity, 0, level] - SHIFT
            one = jnp.broadcast_to(taper[sub : sub + 1, :], (8, LANES))
            one = pltpu.roll(one, (LANES - moved) % LANES, 1)
            wide = jnp.broadcast_to(one[0:1, :], (R, LANES))
            wide = pltpu.roll(wide, 0, 1, stride=1, stride_axis=0)
            window = in_bin - moved
            keep = (window >= 0) & (jnp.abs(window - out_bin) <= 4)
            top = jnp.where(keep, wide[0:edge], 0.0)
            window = window + (R - edge)
            keep = (window < R) & (jnp.abs(window - out_bin) <= 4)
            bottom = jnp.where(keep, wide[R - edge :], 0.0)
            wide = jnp.concatenate([top, wide[edge : R - edge], bottom], axis=0)
            high, low = halves_of(wide)
            at = (2 * level + child, slice(None), pl.ds(parity * LANES, LANES))
            high_ref[at] = high
            low_ref[at] = low


def phase_tables(first_level, count, half, inner_bits, tile, tilt_ref, cos_ref, sin_ref):
    bits = half.bit_length() - 1
    lane = iota((1, LANES), 1)
    angle = jnp.zeros((1, LANES), jnp.float32)
    step = jnp.ones((1, LANES), jnp.float32)
    mask = jnp.zeros((1, LANES), jnp.int32)
    tile_start = jnp.zeros((1, LANES), jnp.int32)
    for level in range(count):
        width = inner_bits + level
        here = (lane >> 2) == level
        step = jnp.where(here, 2.0 ** -(first_level + level), step)
        mask = jnp.where(here, 2**width - 1, mask)
        tile_start = jnp.where(here, tile * 2**width, tile_start)
        for child in range(2):
            angle = jnp.where(
                (lane >> 1) == 2 * level + child, tilt_ref[child, first_level + level], angle
            )
    order = bit_reversed(iota((half, LANES), 0), bits)
    beam = tile_start + (order & mask)
    j_index = (2 * beam + (lane & 1)).astype(jnp.float32)
    phi = angle * ((j_index + 0.5) * step - 1.0)
    norm = 1.0 / math.sqrt(2.0)
    cos_ref[...] = jnp.cos(phi) * norm
    sin_ref[...] = jnp.sin(phi) * norm


def compress_kernel(total_freq, local, echo_ref, matched_hbm, offsets_hbm, fraction_hbm, tilt_hbm,
                    order_hbm, prof_ref, high_ref, low_ref, cos_ref, sin_ref, cos2_ref, sin2_ref,
                    order_ref, table_ref, echo_buf, sum_ref, matched_ref, offsets_ref,
                    fraction_ref, tilt_ref, sems, small_sems):
    pulses, tiles = echo_ref.shape[:2]
    freq = tiles * LANES
    copies = [
        pltpu.make_async_copy(echo_ref.at[:, n], echo_buf.at[n], sems.at[n]) for n in range(tiles)
    ]
    pairs = (
        (matched_hbm, matched_ref),
        (offsets_hbm, offsets_ref),
        (fraction_hbm, fraction_ref),
        (tilt_hbm, tilt_ref),
        (order_hbm, order_ref),
    )
    small = [pltpu.make_async_copy(*pair, small_sems.at[n]) for n, pair in enumerate(pairs)]
    for copy in small + copies:
        copy.start()
    bands, apertures = lax.axis_size("band"), lax.axis_size("aperture")
    band = lax.axis_index("band")
    levels = high_ref.shape[0] // 2
    small[0].wait()
    make_table(total_freq, band * freq, matched_ref, table_ref)
    for copy in small[1:]:
        copy.wait()
    build_matrices(levels, offsets_ref, fraction_ref, high_ref, low_ref)
    phase_tables(0, local, cos_ref.shape[0], 0, 0, tilt_ref, cos_ref, sin_ref)
    devices = bands * apertures
    tile = bit_reversed(lax.axis_index("aperture") * bands + band, devices.bit_length() - 1)
    inner = (pulses // devices).bit_length() - 1
    rest = levels - local
    phase_tables(local, rest, cos2_ref.shape[0], inner, tile, tilt_ref, cos2_ref, sin2_ref)
    for copy in copies:
        copy.wait()
    echoes = jnp.concatenate(
        [echo_buf.at[n].reshape(2 * pulses, LANES)[...] for n in range(tiles)], axis=1
    )
    dims = (((1,), (1,)), ((), ()))
    sums = lax.dot_general(echoes, table_ref[...], dims, preferred_element_type=jnp.float32)
    sum_ref[0] = sums[:, 0:R]
    sum_ref[1] = sums[:, R:]
    even, odd = pl.ds(0, pulses, stride=2), pl.ds(1, pulses, stride=2)
    re = sum_ref[0, even, :] - sum_ref[1, odd, :]
    im = sum_ref[1, even, :] + sum_ref[0, odd, :]
    for part, value in enumerate((re, im)):
        high, low = halves_of(value)
        prof_ref[0:pulses, part * R : (part + 1) * R] = high
        prof_ref[pulses:, part * R : (part + 1) * R] = low


def level_step(level, half, source, tables, high_ref, low_ref):
    cos_ref, sin_ref = tables
    products = []
    for child in range(2):
        held = source[pl.ds(child, 2 * half, stride=2), :]
        high, low = halves_of(held)
        m_high, m_low = high_ref[2 * level + child], low_ref[2 * level + child]
        dot = functools.partial(jnp.dot, preferred_element_type=jnp.float32)
        products.append(dot(high, m_high) + (dot(low, m_high) + dot(high, m_low)))
    result = []
    for parity in range(2):
        re = im = None
        for child in range(2):
            entry = 4 * level + 2 * child + parity
            co = cos_ref[:, entry : entry + 1]
            si = sin_ref[:, entry : entry + 1]
            p_re = products[child][0:half, parity * R : (parity + 1) * R]
            p_im = products[child][half:, parity * R : (parity + 1) * R]
            r_new = p_re * co - p_im * si
            i_new = p_re * si + p_im * co
            re = r_new if re is None else re + r_new
            im = i_new if im is None else im + i_new
        result.append((re, im))
    return result


def local_kernel(count, devices, *refs):
    bands = lax.axis_size("band")
    orders = refs[:bands]
    prof_ref, high_ref, low_ref, cos_ref, sin_ref, out_ref, image_ref = refs[bands:]
    pulses = prof_ref.shape[0] // 2
    half = pulses // 2
    group = pulses // bands
    me = lax.axis_index("band")
    for apart in range(bands):
        start = pl.multiple_of((me ^ apart) * group, group)
        order = orders[apart][...]
        chosen = iota((group, group), 0) == jnp.broadcast_to(order, (group, group))
        chosen = jnp.where(chosen, 1.0, 0.0).astype(jnp.bfloat16)
        twice = jnp.concatenate([chosen, chosen], axis=0)
        held = jnp.concatenate(
            [prof_ref[pl.ds(start, group), :], prof_ref[pl.ds(pulses + start, group), :]], axis=0
        )
        moved = lax.dot_general(
            twice, held, (((0,), (0,)), ((), ())), preferred_element_type=jnp.float32
        )
        image_ref[0, pl.ds(start, group), :] = moved[:, 0:R]
        image_ref[0, pl.ds(pulses + start, group), :] = moved[:, R:]
    kept = pulses // devices
    for level in range(count):
        source, target = image_ref.at[level % 2], image_ref.at[(level + 1) % 2]
        result = level_step(level, half, source, (cos_ref, sin_ref), high_ref, low_ref)
        for parity in range(2):
            for part in range(2):
                value = result[parity][part]
                if level + 1 < count:
                    target[pl.ds(part * pulses + parity * half, half), :] = value
                    continue
                size = min(half, devices)
                for piece in range(half // size):
                    row = parity * half + piece * size
                    begin = (row % devices) * 2 * kept + part * kept + row // devices
                    out_ref[pl.ds(begin, size, stride=2 * kept), :] = value[
                        piece * size : (piece + 1) * size
                    ]


def box(rows):
    total = rows[0]
    for row in rows[1:]:
        total = total + row
    lane = iota(total.shape, 1)
    summed = total
    for off in (1, 2):
        right = pltpu.roll(total, off, 1)
        left = pltpu.roll(total, LANES - off, 1)
        summed = summed + jnp.where(lane >= off, right, 0.0)
        summed = summed + jnp.where(lane < LANES - off, left, 0.0)
    return summed


def near_count(position, size):
    return jnp.minimum(position, 2) + jnp.minimum(size - 1 - position, 2) + 1


def final_kernel(first_level, count, recv_ref, high_ref, low_ref, cos_ref, sin_ref, out_ref,
                 image_ref, pad_ref):
    bands, apertures = lax.axis_size("band"), lax.axis_size("aperture")
    rows = out_ref.shape[0]
    half = rows // 2
    kept = rows // apertures
    high_ref = high_ref.at[2 * first_level : 2 * (first_level + count)]
    low_ref = low_ref.at[2 * first_level : 2 * (first_level + count)]
    for part in range(2):
        for beam in range(kept):
            total = None
            for band in range(bands):
                begin = band * 2 * kept + part * kept + beam
                value = recv_ref[pl.ds(begin, apertures, stride=bands * 2 * kept), :]
                total = value if total is None else total + value
            image_ref[0, pl.ds(part * rows + beam * apertures, apertures), :] = total
    for level in range(count):
        source, target = image_ref.at[level % 2], image_ref.at[(level + 1) % 2]
        result = level_step(level, half, source, (cos_ref, sin_ref), high_ref, low_ref)
        for parity in range(2):
            for part in range(2):
                target[pl.ds(part * rows + parity * half, half), :] = result[parity][part]
    last = image_ref.at[count % 2]
    power = last[0:rows, :] ** 2 + last[rows : 2 * rows, :] ** 2
    image_ref[(count + 1) % 2, 0:rows, :] = power
    edge = 8
    for part in range(2):
        pad_ref[part, 0:edge, :] = jnp.zeros((edge, LANES), jnp.float32)
        pad_ref[part, edge + rows :, :] = jnp.zeros((edge, LANES), jnp.float32)
    bits = rows.bit_length() - 1
    for row in range(rows):
        from_row = bit_reversed(row, bits)
        pad_ref[0, edge + row : edge + row + 1, :] = image_ref[
            (count + 1) % 2, from_row : from_row + 1, :
        ]
    power = pad_ref[0, edge : edge + rows, :]
    pad_ref[1, edge : edge + rows, :] = power * power
    sums = [
        box([pad_ref[part, edge + off : edge + off + rows, :] for off in range(-2, 3)])
        for part in range(2)
    ]
    shape = (rows, LANES)
    cells = near_count(iota(shape, 0), rows) * near_count(iota(shape, 1), LANES)
    cells = cells.astype(jnp.float32)
    mean, square = sums[0] / cells, sums[1] / cells
    gain = (square - mean * mean) / (square - 0.75 * mean * mean + 0.001)
    out_ref[...] = mean + gain * (power - mean)


def body(raw_echoes, pulse_order, matched, offsets, fraction, tilt_angle):
    bands, apertures = lax.axis_size("band"), lax.axis_size("aperture")
    devices = bands * apertures
    pulses, _, freq = raw_echoes.shape
    group = pulse_order.shape[-1]
    levels = tilt_angle.shape[0]
    local = pulses.bit_length() - 1
    rest = levels - local
    kept = pulses // devices
    rows = kept * apertures
    tiles = freq // LANES
    order = pulse_order.reshape(1, group)
    orders = [order]
    for apart in range(1, bands):
        orders.append(lax.ppermute(order, "band", [(n, n ^ apart) for n in range(bands)]))
    vmem = pl.BlockSpec(memory_space=VMEM)
    params = pltpu.CompilerParams(vmem_limit_bytes=16 * 2**20)
    f32, bf16 = jnp.float32, jnp.bfloat16
    shape_of = jax.ShapeDtypeStruct
    views = (
        raw_echoes.reshape(pulses, 2, tiles, LANES).transpose(0, 2, 1, 3),
        matched,
        offsets.transpose(1, 2, 3, 0),
        fraction.transpose(1, 2, 0),
        tilt_angle.transpose(1, 0),
        order,
    )
    views = [pltpu.with_memory_space_constraint(view, pltpu.HBM) for view in views]
    prof, high, low, cos_1, sin_1, cos_2, sin_2, orders[0] = pl.pallas_call(
        functools.partial(compress_kernel, matched.shape[1], local),
        out_shape=[
            shape_of((2 * pulses, 2 * R), bf16),
            shape_of((2 * levels, R, 2 * R), bf16),
            shape_of((2 * levels, R, 2 * R), bf16),
            shape_of((pulses // 2, LANES), f32),
            shape_of((pulses // 2, LANES), f32),
            shape_of((rows // 2, LANES), f32),
            shape_of((rows // 2, LANES), f32),
            shape_of(order.shape, order.dtype),
        ],
        in_specs=[pl.BlockSpec(memory_space=pltpu.HBM)] * 6,
        out_specs=[vmem] * 8,
        scratch_shapes=[
            VMEM((2 * R, freq), bf16),
            VMEM((tiles, pulses, 2, LANES), bf16),
            VMEM((2, 2 * pulses, R), f32),
            VMEM(matched.shape, f32),
            SMEM(views[2].shape, jnp.int32),
            SMEM(views[3].shape, f32),
            SMEM(views[4].shape, f32),
            pltpu.SemaphoreType.DMA((tiles,)),
            pltpu.SemaphoreType.DMA((5,)),
        ],
        cost_estimate=pl.CostEstimate(
            flops=8 * pulses * freq * R, bytes_accessed=4 * pulses * freq, transcendentals=0
        ),
        compiler_params=params,
        name="compress",
    )(*views)
    sent = pl.pallas_call(
        functools.partial(local_kernel, local, devices),
        out_shape=shape_of((devices * 2 * kept, R), f32),
        in_specs=[vmem] * (bands + 5),
        out_specs=vmem,
        scratch_shapes=[VMEM((2, 2 * pulses, R), f32)],
        compiler_params=params,
        name="levels",
    )(*orders, prof, high, low, cos_1, sin_1)
    received = lax.all_to_all(
        sent.reshape(devices, 2 * kept, R), ("aperture", "band"), 0, 0, tiled=True
    ).reshape(devices * 2 * kept, R)
    return pl.pallas_call(
        functools.partial(final_kernel, local, rest),
        out_shape=shape_of((rows, R), f32),
        in_specs=[vmem] * 5,
        out_specs=vmem,
        scratch_shapes=[VMEM((2, 2 * rows, R), f32), VMEM((2, rows + 16, R), f32)],
        compiler_params=params,
        name="finish",
    )(received, high, low, cos_2, sin_2)


def solution(mesh):
    in_specs = (P("aperture", None, "band"), P("aperture", "band", None), P(), P(), P(), P())
    out_specs = P(("band", "aperture"), None)
    return jax.shard_map(body, mesh=mesh, in_specs=in_specs, out_specs=out_specs, check_vma=False)
```

```python
import functools
import math

import jax
import jax.numpy as jnp
from jax import lax
from jax.experimental import pallas as pl
from jax.experimental.pallas import tpu as pltpu
from jax.sharding import PartitionSpec as P

R = 128
SHIFT = 8
LANES = 128
VMEM = pltpu.VMEM
SMEM = pltpu.SMEM


def iota(shape, axis):
    return lax.broadcasted_iota(jnp.int32, shape, axis)


def bit_reversed(value, bits):
    result = value & 0
    for bit in range(bits):
        result = result | (((value >> bit) & 1) << (bits - 1 - bit))
    return result


def halves_of(value):
    high = value.astype(jnp.bfloat16)
    low = (value - high.astype(jnp.float32)).astype(jnp.bfloat16)
    return high, low


def cmul(first, second):
    return (
        first[0] * second[0] - first[1] * second[1],
        first[0] * second[1] + first[1] * second[0],
    )


def make_table(total_freq, start, matched_ref, table_ref):
    chunks = table_ref.shape[0]
    scale = 1.0 / math.sqrt(total_freq)
    turn = 2.0 * math.pi / total_freq
    rows = -(-chunks // 8) * 8
    f_index = start + iota((rows, LANES), 0) * LANES + iota((rows, LANES), 1)
    angle = f_index.astype(jnp.float32) * turn
    cos_1, sin_1 = jnp.cos(angle), jnp.sin(angle)
    sub = iota((8, LANES), 0)
    for chunk in range(chunks):
        lanes = pl.ds(pl.multiple_of(start + chunk * LANES, LANES), LANES)
        power = [
            jnp.broadcast_to(part[chunk : chunk + 1, :], (8, LANES)) for part in (cos_1, sin_1)
        ]
        spec = matched_ref[:, lanes] * scale
        low = tuple(jnp.broadcast_to(spec[n : n + 1, :], (8, LANES)) for n in range(2))
        for bit in range(3):
            chosen = (sub >> bit) & 1 == 1
            low = cmul(low, (jnp.where(chosen, power[0], 1.0), jnp.where(chosen, power[1], 0.0)))
            power = cmul(power, power)
        block = [jnp.concatenate(parts, axis=0) for parts in zip(low, cmul(low, power))]
        power = cmul(power, power)
        power = [jnp.concatenate([part, part], axis=0) for part in power]
        for begin in range(0, R, 16):
            table_ref[chunk, begin : begin + 16, :] = block[0].astype(jnp.bfloat16)
            table_ref[chunk, R + begin : R + begin + 16, :] = block[1].astype(jnp.bfloat16)
            if begin + 16 < R:
                block = cmul(block, power)


def build_matrices(levels, offsets_ref, fraction_ref, start_ref, band_ref, high_ref, low_ref):
    period = 4 * SHIFT
    lane, row = iota((8, LANES), 1), iota((8, LANES), 0)
    near_tap = lane & (period - 1)
    tap = jnp.where(near_tap < period // 2, -near_tap, period - near_tap).astype(jnp.float32)
    entries = [(n, c, p) for n in range(levels) for c in range(2) for p in range(2)]
    for block in range(0, len(entries), 8):
        here = entries[block : block + 8]
        shift = jnp.zeros((8, LANES), jnp.float32)
        for sub, (level, child, parity) in enumerate(here):
            shift = jnp.where(row == sub, fraction_ref[child, parity, level], shift)
        dist = tap - shift
        turn = math.pi * dist
        near = jnp.abs(dist) < 1e-12
        sinc = jnp.where(near, 1.0, jnp.sin(turn) / jnp.where(near, 1.0, turn))
        taper = sinc * jnp.exp(-((dist / 2.5) ** 2))
        taper = jnp.where(jnp.abs(dist) <= 4.0, taper, 0.0)
        for sub, (level, child, parity) in enumerate(here):
            moved = offsets_ref[child, parity, 0, level] - SHIFT
            one = jnp.broadcast_to(taper[sub : sub + 1, :], (8, LANES))
            one = pltpu.roll(one, (LANES - moved) & (LANES - 1), 1)
            start_ref[block + sub] = pltpu.roll(one, 0, 1, stride=1, stride_axis=0)
    for begin in range(0, R, 8):
        first = begin - SHIFT - 4
        inside = (lane >= first) & (lane < first + period)
        band_ref[begin // 8] = jnp.where(inside, 1.0, 0.0)
    for entry, (level, child, parity) in enumerate(entries):
        moved = offsets_ref[child, parity, 0, level] - SHIFT
        one = start_ref[entry]
        turned = [one] + [pltpu.roll(one, begin, 1) for begin in range(8, period, 8)]
        halves = []
        for value in turned:
            high = value.astype(jnp.bfloat16).astype(jnp.float32)
            halves.append((high, value - high))
        first = jnp.where(row >= moved, band_ref[0], 0.0)
        last = jnp.where(row < moved + 8, band_ref[R // 8 - 1], 0.0)
        for begin in range(0, R, 16):
            for part, ref in enumerate((high_ref, low_ref)):
                tiles = []
                for tile in (begin // 8, begin // 8 + 1):
                    keep = first if tile == 0 else last if tile == R // 8 - 1 else band_ref[tile]
                    tiles.append(halves[tile % len(halves)][part] * keep)
                ref[entry, begin : begin + 16, :] = jnp.concatenate(tiles, 0).astype(jnp.bfloat16)


def phase_tables(first_level, count, inner_bits, tile, tilt_ref, cos_ref, sin_ref):
    half = cos_ref.shape[0]
    bits = half.bit_length() - 1
    lane = iota((1, LANES), 1)
    angle = jnp.zeros((1, LANES), jnp.float32)
    step = jnp.ones((1, LANES), jnp.float32)
    mask = jnp.zeros((1, LANES), jnp.int32)
    tile_start = jnp.zeros((1, LANES), jnp.int32)
    for level in range(count):
        width = inner_bits + level
        here = (lane >> 2) == level
        step = jnp.where(here, 2.0 ** -(first_level + level), step)
        mask = jnp.where(here, 2**width - 1, mask)
        tile_start = jnp.where(here, tile * 2**width, tile_start)
        for child in range(2):
            angle = jnp.where(
                (lane >> 1) == 2 * level + child, tilt_ref[child, first_level + level], angle
            )
    norm = 1.0 / math.sqrt(2.0)
    beam = tile_start + (bit_reversed(iota((8, LANES), 0), bits) & mask)
    j_index = (2 * beam + (lane & 1)).astype(jnp.float32)
    phi = angle * ((j_index + 0.5) * step - 1.0)
    inner = (jnp.cos(phi) * norm, jnp.sin(phi) * norm)
    groups = half // 8
    shape = (-(-groups // 8) * 8, LANES)
    beam = bit_reversed(iota(shape, 0) << 3, bits) & mask
    phi = angle * ((2 * beam).astype(jnp.float32) * step)
    outer = (jnp.cos(phi), jnp.sin(phi))
    for group in range(groups):
        co, si = cmul(inner, [part[group : group + 1, :] for part in outer])
        cos_ref[8 * group : 8 * group + 8, :] = co
        sin_ref[8 * group : 8 * group + 8, :] = si


def compress_kernel(total_freq, local, echo_ref, matched_hbm, offsets_hbm, fraction_hbm, tilt_hbm,
                    order_hbm, prof_ref, high_ref, low_ref, cos_ref, sin_ref, cos2_ref, sin2_ref,
                    order_ref, table_ref, echo_buf, line_buf, sum_ref, start_ref, band_ref, matched_ref, offsets_ref,
                    fraction_ref, tilt_ref, sems, line_sems, small_sems):
    pulses, tiles = echo_ref.shape[:2]
    freq = tiles * LANES
    copies = [
        pltpu.make_async_copy(echo_ref.at[:, n], echo_buf.at[n], sems.at[n]) for n in range(tiles)
    ]
    pairs = (
        (matched_hbm, matched_ref),
        (offsets_hbm, offsets_ref),
        (fraction_hbm, fraction_ref),
        (tilt_hbm, tilt_ref),
        (order_hbm, order_ref),
    )
    small = [pltpu.make_async_copy(*pair, small_sems.at[n]) for n, pair in enumerate(pairs)]
    for copy in small + copies:
        copy.start()
    bands, apertures = lax.axis_size("band"), lax.axis_size("aperture")
    band = lax.axis_index("band")
    levels = high_ref.shape[0] // 4
    small[0].wait()
    make_table(total_freq, band * freq, matched_ref, table_ref)
    for copy in small[1:] + copies:
        copy.wait()
    copies = [
        pltpu.make_async_copy(
            echo_buf.at[n].reshape(2 * pulses, LANES), line_buf.at[n], line_sems.at[n]
        )
        for n in range(tiles)
    ]
    for copy in copies:
        copy.start()
    build_matrices(levels, offsets_ref, fraction_ref, start_ref, band_ref, high_ref, low_ref)
    phase_tables(0, local, 0, 0, tilt_ref, cos_ref, sin_ref)
    devices = bands * apertures
    tile = bit_reversed(lax.axis_index("aperture") * bands + band, devices.bit_length() - 1)
    inner = (pulses // devices).bit_length() - 1
    rest = levels - local
    phase_tables(local, rest, inner, tile, tilt_ref, cos2_ref, sin2_ref)
    for copy in copies:
        copy.wait()
    echoes = jnp.concatenate([line_buf[n] for n in range(tiles)], axis=1)
    dims = (((1,), (1,)), ((), ()))
    table = jnp.concatenate([table_ref[n] for n in range(tiles)], axis=1)
    sums = lax.dot_general(echoes, table, dims, preferred_element_type=jnp.float32)
    sum_ref[0] = sums[:, 0:R]
    sum_ref[1] = sums[:, R:]
    even, odd = pl.ds(0, pulses, stride=2), pl.ds(1, pulses, stride=2)
    re = sum_ref[0, even, :] - sum_ref[1, odd, :]
    im = sum_ref[1, even, :] + sum_ref[0, odd, :]
    for part, value in enumerate((re, im)):
        high, low = halves_of(value)
        prof_ref[part, 0:pulses, :] = high
        prof_ref[part, pulses:, :] = low


def level_step(level, half, source, tables, high_ref, low_ref):
    cos_ref, sin_ref = tables
    products = []
    for child in range(2):
        held = source[pl.ds(child, 2 * half, stride=2), :]
        high, low = halves_of(held)
        at = 4 * level + 2 * child
        m_high, m_low = (
            jnp.concatenate([ref[at], ref[at + 1]], axis=1) for ref in (high_ref, low_ref)
        )
        dot = functools.partial(jnp.dot, preferred_element_type=jnp.float32)
        both = jnp.concatenate([high, low], axis=1)
        m_both = jnp.concatenate([m_high, m_high], axis=0)
        products.append(dot(both, m_both) + dot(high, m_low))
    result = []
    for parity in range(2):
        re = im = None
        for child in range(2):
            entry = 4 * level + 2 * child + parity
            co = cos_ref[:, entry : entry + 1]
            si = sin_ref[:, entry : entry + 1]
            p_re = products[child][0:half, parity * R : (parity + 1) * R]
            p_im = products[child][half:, parity * R : (parity + 1) * R]
            r_new = p_re * co - p_im * si
            i_new = p_re * si + p_im * co
            re = r_new if re is None else re + r_new
            im = i_new if im is None else im + i_new
        result.append((re, im))
    return result


def local_kernel(count, devices, *refs):
    bands = lax.axis_size("band")
    orders = refs[:bands]
    prof_ref, high_ref, low_ref, cos_ref, sin_ref, out_ref, image_ref = refs[bands:]
    pulses = prof_ref.shape[1] // 2
    half = pulses // 2
    group = pulses // bands
    me = lax.axis_index("band")
    for apart in range(bands):
        start = pl.multiple_of((me ^ apart) * group, group)
        order = orders[apart][...]
        chosen = iota((group, group), 0) == jnp.broadcast_to(order, (group, group))
        chosen = jnp.where(chosen, 1.0, 0.0).astype(jnp.bfloat16)
        twice = jnp.concatenate([chosen, chosen], axis=0)
        held = jnp.concatenate(
            [
                jnp.concatenate(
                    [prof_ref[part, pl.ds(side + start, group), :] for side in (0, pulses)], axis=0
                )
                for part in range(2)
            ],
            axis=1,
        )
        moved = lax.dot_general(
            twice, held, (((0,), (0,)), ((), ())), preferred_element_type=jnp.float32
        )
        image_ref[0, pl.ds(start, group), :] = moved[:, 0:R]
        image_ref[0, pl.ds(pulses + start, group), :] = moved[:, R:]
    kept = pulses // devices
    for level in range(count):
        source, target = image_ref.at[level % 2], image_ref.at[(level + 1) % 2]
        result = level_step(level, half, source, (cos_ref, sin_ref), high_ref, low_ref)
        for parity in range(2):
            for part in range(2):
                value = result[parity][part]
                if level + 1 < count:
                    target[pl.ds(part * pulses + parity * half, half), :] = value
                    continue
                size = min(half, devices)
                for piece in range(half // size):
                    row = parity * half + piece * size
                    begin = (row % devices) * 2 * kept + part * kept + row // devices
                    out_ref[pl.ds(begin, size, stride=2 * kept), :] = value[
                        piece * size : (piece + 1) * size
                    ]


def box(rows):
    total = rows[0]
    for row in rows[1:]:
        total = total + row
    lane = iota(total.shape, 1)
    summed = total
    for off in (1, 2):
        right = pltpu.roll(total, off, 1)
        left = pltpu.roll(total, LANES - off, 1)
        summed = summed + jnp.where(lane >= off, right, 0.0)
        summed = summed + jnp.where(lane < LANES - off, left, 0.0)
    return summed


def near_count(position, size):
    return jnp.minimum(position, 2) + jnp.minimum(size - 1 - position, 2) + 1


def final_kernel(first_level, count, recv_ref, high_ref, low_ref, cos_ref, sin_ref, out_ref,
                 image_ref, pad_ref):
    bands, apertures = lax.axis_size("band"), lax.axis_size("aperture")
    rows = out_ref.shape[0]
    half = rows // 2
    kept = rows // apertures
    high_ref = high_ref.at[4 * first_level : 4 * (first_level + count)]
    low_ref = low_ref.at[4 * first_level : 4 * (first_level + count)]
    for part in range(2):
        for beam in range(kept):
            total = None
            for band in range(bands):
                begin = band * 2 * kept + part * kept + beam
                value = recv_ref[pl.ds(begin, apertures, stride=bands * 2 * kept), :]
                total = value if total is None else total + value
            image_ref[0, pl.ds(part * rows + beam * apertures, apertures), :] = total
    for level in range(count):
        source, target = image_ref.at[level % 2], image_ref.at[(level + 1) % 2]
        result = level_step(level, half, source, (cos_ref, sin_ref), high_ref, low_ref)
        for parity in range(2):
            for part in range(2):
                target[pl.ds(part * rows + parity * half, half), :] = result[parity][part]
    last = image_ref.at[count % 2]
    power = last[0:rows, :] ** 2 + last[rows : 2 * rows, :] ** 2
    image_ref[(count + 1) % 2, 0:rows, :] = power
    edge = 8
    for part in range(2):
        pad_ref[part, 0:edge, :] = jnp.zeros((edge, LANES), jnp.float32)
        pad_ref[part, edge + rows :, :] = jnp.zeros((edge, LANES), jnp.float32)
    bits = rows.bit_length() - 1
    for row in range(rows):
        from_row = bit_reversed(row, bits)
        pad_ref[0, edge + row : edge + row + 1, :] = image_ref[
            (count + 1) % 2, from_row : from_row + 1, :
        ]
    power = pad_ref[0, edge : edge + rows, :]
    pad_ref[1, edge : edge + rows, :] = power * power
    sums = [
        box([pad_ref[part, edge + off : edge + off + rows, :] for off in range(-2, 3)])
        for part in range(2)
    ]
    shape = (rows, LANES)
    cells = near_count(iota(shape, 0), rows) * near_count(iota(shape, 1), LANES)
    cells = cells.astype(jnp.float32)
    mean, square = sums[0] / cells, sums[1] / cells
    gain = (square - mean * mean) / (square - 0.75 * mean * mean + 0.001)
    out_ref[...] = mean + gain * (power - mean)


def body(raw_echoes, pulse_order, matched, offsets, fraction, tilt_angle):
    bands, apertures = lax.axis_size("band"), lax.axis_size("aperture")
    devices = bands * apertures
    pulses, _, freq = raw_echoes.shape
    group = pulse_order.shape[-1]
    levels = tilt_angle.shape[0]
    local = pulses.bit_length() - 1
    rest = levels - local
    kept = pulses // devices
    rows = kept * apertures
    tiles = freq // LANES
    order = pulse_order.reshape(1, group)
    orders = [order]
    for apart in range(1, bands):
        orders.append(lax.ppermute(order, "band", [(n, n ^ apart) for n in range(bands)]))
    vmem = pl.BlockSpec(memory_space=VMEM)
    params = pltpu.CompilerParams(vmem_limit_bytes=16 * 2**20)
    f32, bf16 = jnp.float32, jnp.bfloat16
    shape_of = jax.ShapeDtypeStruct
    views = (
        raw_echoes.reshape(pulses, 2, tiles, LANES).transpose(0, 2, 1, 3),
        matched,
        offsets.transpose(1, 2, 3, 0),
        fraction.transpose(1, 2, 0),
        tilt_angle.transpose(1, 0),
        order,
    )
    views = [pltpu.with_memory_space_constraint(view, pltpu.HBM) for view in views]
    prof, high, low, cos_1, sin_1, cos_2, sin_2, orders[0] = pl.pallas_call(
        functools.partial(compress_kernel, matched.shape[1], local),
        out_shape=[
            shape_of((2, 2 * pulses, R), bf16),
            shape_of((4 * levels, R, R), bf16),
            shape_of((4 * levels, R, R), bf16),
            shape_of((pulses // 2, LANES), f32),
            shape_of((pulses // 2, LANES), f32),
            shape_of((rows // 2, LANES), f32),
            shape_of((rows // 2, LANES), f32),
            shape_of(order.shape, order.dtype),
        ],
        in_specs=[pl.BlockSpec(memory_space=pltpu.HBM)] * 6,
        out_specs=[vmem] * 8,
        scratch_shapes=[
            VMEM((tiles, 2 * R, LANES), bf16),
            VMEM((tiles, pulses, 2, LANES), bf16),
            VMEM((tiles, 2 * pulses, LANES), bf16),
            VMEM((2, 2 * pulses, R), f32),
            VMEM((4 * levels, 8, LANES), f32),
            VMEM((R // 8, 8, LANES), f32),
            VMEM(matched.shape, f32),
            SMEM(views[2].shape, jnp.int32),
            SMEM(views[3].shape, f32),
            SMEM(views[4].shape, f32),
            pltpu.SemaphoreType.DMA((tiles,)),
            pltpu.SemaphoreType.DMA((tiles,)),
            pltpu.SemaphoreType.DMA((5,)),
        ],
        cost_estimate=pl.CostEstimate(
            flops=8 * pulses * freq * R, bytes_accessed=4 * pulses * freq, transcendentals=0
        ),
        compiler_params=params,
        name="compress",
    )(*views)
    sent = pl.pallas_call(
        functools.partial(local_kernel, local, devices),
        out_shape=shape_of((devices * 2 * kept, R), f32),
        in_specs=[vmem] * (bands + 5),
        out_specs=vmem,
        scratch_shapes=[VMEM((2, 2 * pulses, R), f32)],
        compiler_params=params,
        name="levels",
    )(*orders, prof, high, low, cos_1, sin_1)
    received = lax.all_to_all(
        sent.reshape(devices, 2 * kept, R), ("aperture", "band"), 0, 0, tiled=True
    ).reshape(devices * 2 * kept, R)
    return pl.pallas_call(
        functools.partial(final_kernel, local, rest),
        out_shape=shape_of((rows, R), f32),
        in_specs=[vmem] * 5,
        out_specs=vmem,
        scratch_shapes=[VMEM((2, 2 * rows, R), f32), VMEM((2, rows + 16, R), f32)],
        compiler_params=params,
        name="finish",
    )(received, high, low, cos_2, sin_2)


def solution(mesh):
    in_specs = (P("aperture", None, "band"), P("aperture", "band", None), P(), P(), P(), P())
    out_specs = P(("band", "aperture"), None)
    return jax.shard_map(body, mesh=mesh, in_specs=in_specs, out_specs=out_specs, check_vma=False)
```

```python
import functools
import math

import jax
import jax.numpy as jnp
from jax import lax
from jax.experimental import pallas as pl
from jax.experimental.pallas import tpu as pltpu
from jax.sharding import PartitionSpec as P

R = 128
SHIFT = 8
LANES = 128
VMEM = pltpu.VMEM
SMEM = pltpu.SMEM


def iota(shape, axis):
    return lax.broadcasted_iota(jnp.int32, shape, axis)


def bit_reversed(value, bits):
    result = value & 0
    for bit in range(bits):
        result = result | (((value >> bit) & 1) << (bits - 1 - bit))
    return result


def halves_of(value):
    high = value.astype(jnp.bfloat16)
    low = (value - high.astype(jnp.float32)).astype(jnp.bfloat16)
    return high, low


def cmul(first, second):
    return (
        first[0] * second[0] - first[1] * second[1],
        first[0] * second[1] + first[1] * second[0],
    )


def unit_table(total_freq, start, chunks):
    turn = 2.0 * math.pi / total_freq
    rows = -(-chunks // 8) * 8
    f_index = start + iota((rows, LANES), 0) * LANES + iota((rows, LANES), 1)
    angle = f_index.astype(jnp.float32) * turn
    return jnp.cos(angle), jnp.sin(angle)


def make_table(total_freq, start, twiddles, matched_ref, table_ref):
    chunks = table_ref.shape[0]
    scale = 1.0 / math.sqrt(total_freq)
    cos_1, sin_1 = twiddles
    sub = iota((8, LANES), 0)
    for chunk in range(chunks):
        lanes = pl.ds(pl.multiple_of(start + chunk * LANES, LANES), LANES)
        power = [
            jnp.broadcast_to(part[chunk : chunk + 1, :], (8, LANES)) for part in (cos_1, sin_1)
        ]
        spec = matched_ref[:, lanes] * scale
        low = tuple(jnp.broadcast_to(spec[n : n + 1, :], (8, LANES)) for n in range(2))
        for bit in range(3):
            chosen = (sub >> bit) & 1 == 1
            low = cmul(low, (jnp.where(chosen, power[0], 1.0), jnp.where(chosen, power[1], 0.0)))
            power = cmul(power, power)
        block = [jnp.concatenate(parts, axis=0) for parts in zip(low, cmul(low, power))]
        power = cmul(power, power)
        power = [jnp.concatenate([part, part], axis=0) for part in power]
        for begin in range(0, R, 16):
            table_ref[chunk, begin : begin + 16, :] = block[0].astype(jnp.bfloat16)
            table_ref[chunk, R + begin : R + begin + 16, :] = block[1].astype(jnp.bfloat16)
            if begin + 16 < R:
                block = cmul(block, power)


def edge_bands():
    lane = iota((8, LANES), 1)
    period = 4 * SHIFT
    result = []
    for begin in range(0, R, 8):
        first = begin - SHIFT - 4
        result.append(jnp.where((lane >= first) & (lane < first + period), 1.0, 0.0))
    return result


def build_starts(levels, offsets_ref, fraction_ref, start_ref, edge_ref):
    period = 4 * SHIFT
    lane, row = iota((8, LANES), 1), iota((8, LANES), 0)
    near_tap = lane & (period - 1)
    tap = jnp.where(near_tap < period // 2, -near_tap, period - near_tap).astype(jnp.float32)
    bands = edge_bands()
    entries = [(n, c, p) for n in range(levels) for c in range(2) for p in range(2)]
    for block in range(0, len(entries), 8):
        here = entries[block : block + 8]
        shift = jnp.zeros((8, LANES), jnp.float32)
        for sub, (level, child, parity) in enumerate(here):
            shift = jnp.where(row == sub, fraction_ref[child, parity, level], shift)
        dist = tap - shift
        turn = math.pi * dist
        near = jnp.abs(dist) < 1e-12
        sinc = jnp.where(near, 1.0, jnp.sin(turn) / jnp.where(near, 1.0, turn))
        taper = sinc * jnp.exp(-((dist / 2.5) ** 2))
        taper = jnp.where(jnp.abs(dist) <= 4.0, taper, 0.0)
        for sub, (level, child, parity) in enumerate(here):
            moved = offsets_ref[child, parity, 0, level] - SHIFT
            one = jnp.broadcast_to(taper[sub : sub + 1, :], (8, LANES))
            one = pltpu.roll(one, (LANES - moved) & (LANES - 1), 1)
            start_ref[block + sub] = pltpu.roll(one, 0, 1, stride=1, stride_axis=0)
            edge_ref[0, block + sub] = jnp.where(row >= moved, bands[0], 0.0)
            edge_ref[1, block + sub] = jnp.where(row < moved + 8, bands[-1], 0.0)


def build_angles(first_level, count, tilt_ref):
    lane = iota((1, LANES), 1)
    angle = jnp.zeros((1, LANES), jnp.float32)
    for level in range(count):
        for child in range(2):
            angle = jnp.where(
                (lane >> 1) == 2 * level + child, tilt_ref[child, first_level + level], angle
            )
    return angle


def build_matrices(start_ref, edge_ref, band_ref, high_ref, low_ref):
    period = 4 * SHIFT
    for tile, band in enumerate(edge_bands()):
        band_ref[tile] = band
    last = R // 8 - 1
    for entry in range(start_ref.shape[0]):
        one = start_ref[entry]
        turned = [one] + [pltpu.roll(one, begin, 1) for begin in range(8, period, 8)]
        halves = []
        for value in turned:
            high = value.astype(jnp.bfloat16).astype(jnp.float32)
            halves.append((high, value - high))
        for begin in range(0, R, 16):
            for part, ref in enumerate((high_ref, low_ref)):
                tiles = []
                for tile in (begin // 8, begin // 8 + 1):
                    if tile in (0, last):
                        keep = edge_ref[tile // last, entry]
                    else:
                        keep = band_ref[tile]
                    tiles.append(halves[tile % len(halves)][part] * keep)
                ref[entry, begin : begin + 16, :] = jnp.concatenate(tiles, 0).astype(jnp.bfloat16)


def phase_tables(first_level, count, inner_bits, tile, angle, cos_ref, sin_ref):
    half = cos_ref.shape[0]
    bits = half.bit_length() - 1
    lane = iota((1, LANES), 1)
    step = jnp.ones((1, LANES), jnp.float32)
    mask = jnp.zeros((1, LANES), jnp.int32)
    tile_start = jnp.zeros((1, LANES), jnp.int32)
    for level in range(count):
        width = inner_bits + level
        here = (lane >> 2) == level
        step = jnp.where(here, 2.0 ** -(first_level + level), step)
        mask = jnp.where(here, 2**width - 1, mask)
        tile_start = jnp.where(here, tile * 2**width, tile_start)
    norm = 1.0 / math.sqrt(2.0)
    beam = tile_start + (bit_reversed(iota((8, LANES), 0), bits) & mask)
    j_index = (2 * beam + (lane & 1)).astype(jnp.float32)
    phi = angle * ((j_index + 0.5) * step - 1.0)
    inner = (jnp.cos(phi) * norm, jnp.sin(phi) * norm)
    groups = half // 8
    shape = (-(-groups // 8) * 8, LANES)
    beam = bit_reversed(iota(shape, 0) << 3, bits) & mask
    phi = angle * ((2 * beam).astype(jnp.float32) * step)
    outer = (jnp.cos(phi), jnp.sin(phi))
    for group in range(groups):
        co, si = cmul(inner, [part[group : group + 1, :] for part in outer])
        cos_ref[8 * group : 8 * group + 8, :] = co
        sin_ref[8 * group : 8 * group + 8, :] = si


def compress_kernel(total_freq, local, fold, *refs):
    echo_ref, matched_hbm, offsets_hbm, fraction_hbm, tilt_hbm, order_hbm = refs[:6]
    shares, refs = refs[6 : 6 + fold], refs[6 + fold :]
    start_ref, edge_ref, angle_ref, order_ref = refs[:4]
    table_ref, echo_buf, line_buf, sum_ref, matched_ref = refs[4:9]
    offsets_ref, fraction_ref, tilt_ref, sems, line_sems, small_sems = refs[9:]
    pulses, tiles = echo_ref.shape[:2]
    freq = tiles * LANES
    copies = [
        pltpu.make_async_copy(echo_ref.at[:, n], echo_buf.at[n], sems.at[n]) for n in range(tiles)
    ]
    pairs = (
        (matched_hbm, matched_ref),
        (offsets_hbm, offsets_ref),
        (fraction_hbm, fraction_ref),
        (tilt_hbm, tilt_ref),
        (order_hbm, order_ref),
    )
    small = [pltpu.make_async_copy(*pair, small_sems.at[n]) for n, pair in enumerate(pairs)]
    for copy in small + copies:
        copy.start()
    bands = lax.axis_size("band")
    band = lax.axis_index("band")
    levels = start_ref.shape[0] // 4
    twiddles = unit_table(total_freq, band * freq, tiles)
    for copy in small[1:]:
        copy.wait()
    build_starts(levels, offsets_ref, fraction_ref, start_ref, edge_ref)
    angle_ref[0:1, :] = build_angles(0, local, tilt_ref)
    angle_ref[1:2, :] = build_angles(local, levels - local, tilt_ref)
    for copy in copies:
        copy.wait()
    copies = [
        pltpu.make_async_copy(
            echo_buf.at[n].reshape(2 * pulses, LANES), line_buf.at[n], line_sems.at[n]
        )
        for n in range(tiles)
    ]
    for copy in copies:
        copy.start()
    small[0].wait()
    make_table(total_freq, band * freq, twiddles, matched_ref, table_ref)
    for copy in copies:
        copy.wait()
    echoes = jnp.concatenate([line_buf[n] for n in range(tiles)], axis=1)
    dims = (((1,), (1,)), ((), ()))
    table = jnp.concatenate([table_ref[n] for n in range(tiles)], axis=1)
    sums = lax.dot_general(echoes, table, dims, preferred_element_type=jnp.float32)
    sum_ref[0] = sums[:, 0:R]
    sum_ref[1] = sums[:, R:]
    group = pulses // bands
    held = bands // fold
    for side in range(fold):
        for member in range(held):
            first = 2 * group * (member * fold + ((band ^ side) & (fold - 1)))
            even = pl.ds(pl.multiple_of(first, 8), group, stride=2)
            odd = pl.ds(first + 1, group, stride=2)
            re = sum_ref[0, even, :] - sum_ref[1, odd, :]
            im = sum_ref[1, even, :] + sum_ref[0, odd, :]
            shares[side][0, member * group : (member + 1) * group, :] = re
            shares[side][1, member * group : (member + 1) * group, :] = im


def matrix_kernel(local, inner, start_ref, edge_ref, angle_ref, high_ref, low_ref,
                  cos_ref, sin_ref, cos2_ref, sin2_ref, band_ref):
    bands, apertures = lax.axis_size("band"), lax.axis_size("aperture")
    levels = start_ref.shape[0] // 4
    build_matrices(start_ref, edge_ref, band_ref, high_ref, low_ref)
    phase_tables(0, local, 0, 0, angle_ref[0:1, :], cos_ref, sin_ref)
    place = lax.axis_index("aperture") * bands + lax.axis_index("band")
    tile = bit_reversed(place, (bands * apertures).bit_length() - 1)
    phase_tables(local, levels - local, inner, tile, angle_ref[1:2, :], cos2_ref, sin2_ref)


def level_step(level, half, source, tables, high_ref, low_ref):
    cos_ref, sin_ref = tables
    products = []
    for child in range(2):
        held = source[pl.ds(child, 2 * half, stride=2), :]
        high, low = halves_of(held)
        at = 4 * level + 2 * child
        m_high, m_low = (
            jnp.concatenate([ref[at], ref[at + 1]], axis=1) for ref in (high_ref, low_ref)
        )
        dot = functools.partial(jnp.dot, preferred_element_type=jnp.float32)
        both = jnp.concatenate([high, low], axis=1)
        m_both = jnp.concatenate([m_high, m_high], axis=0)
        products.append(dot(both, m_both) + dot(high, m_low))
    result = []
    for parity in range(2):
        re = im = None
        for child in range(2):
            entry = 4 * level + 2 * child + parity
            co = cos_ref[:, entry : entry + 1]
            si = sin_ref[:, entry : entry + 1]
            p_re = products[child][0:half, parity * R : (parity + 1) * R]
            p_im = products[child][half:, parity * R : (parity + 1) * R]
            r_new = p_re * co - p_im * si
            i_new = p_re * si + p_im * co
            re = r_new if re is None else re + r_new
            im = i_new if im is None else im + i_new
        result.append((re, im))
    return result


def local_kernel(count, fold, *refs):
    devices = lax.axis_size("band") * lax.axis_size("aperture")
    held = lax.axis_size("band") // fold
    orders, shares, refs = refs[:held], refs[held : held + fold], refs[held + fold :]
    high_ref, low_ref, cos_ref, sin_ref, out_ref, image_ref = refs
    rows = shares[0].shape[1]
    half = rows // 2
    group = rows // held
    me = lax.axis_index("band") // fold
    for apart in range(held):
        start = pl.multiple_of((me ^ apart) * group, group)
        chosen = iota((group, group), 0) == jnp.broadcast_to(orders[apart][...], (group, group))
        chosen = jnp.where(chosen, 1.0, 0.0).astype(jnp.bfloat16)
        twice = jnp.concatenate([chosen, chosen], axis=0)
        parts = []
        for part in range(2):
            value = shares[0][part, pl.ds(start, group), :]
            for share in shares[1:]:
                value = value + share[part, pl.ds(start, group), :]
            parts.append(jnp.concatenate(halves_of(value), axis=0))
        moved = lax.dot_general(
            twice,
            jnp.concatenate(parts, axis=1),
            (((0,), (0,)), ((), ())),
            preferred_element_type=jnp.float32,
        )
        image_ref[0, pl.ds(start, group), :] = moved[:, 0:R]
        image_ref[0, pl.ds(rows + start, group), :] = moved[:, R:]
    for level in range(count):
        source, target = image_ref.at[level % 2], image_ref.at[(level + 1) % 2]
        result = level_step(level, half, source, (cos_ref, sin_ref), high_ref, low_ref)
        for parity in range(2):
            for part in range(2):
                target[pl.ds(part * rows + parity * half, half), :] = result[parity][part]
    last = image_ref.at[count % 2]
    per = rows // devices
    for part in range(2):
        for unit in range(per):
            if fold == 1:
                value = last[pl.ds(part * rows + unit * devices, devices), :]
            else:
                value = last[pl.ds(part * rows + unit, devices, stride=per), :]
            out_ref[pl.ds(part * per + unit, devices, stride=2 * per), :] = value


def box(rows):
    total = rows[0]
    for row in rows[1:]:
        total = total + row
    lane = iota(total.shape, 1)
    summed = total
    for off in (1, 2):
        right = pltpu.roll(total, off, 1)
        left = pltpu.roll(total, LANES - off, 1)
        summed = summed + jnp.where(lane >= off, right, 0.0)
        summed = summed + jnp.where(lane < LANES - off, left, 0.0)
    return summed


def near_count(position, size):
    return jnp.minimum(position, 2) + jnp.minimum(size - 1 - position, 2) + 1


def final_kernel(first_level, count, fold, recv_ref, high_ref, low_ref, cos_ref, sin_ref, out_ref,
                 image_ref, pad_ref):
    bands, apertures = lax.axis_size("band"), lax.axis_size("aperture")
    rows = out_ref.shape[0]
    half = rows // 2
    per = recv_ref.shape[0] // (2 * bands * apertures)
    high_ref = high_ref.at[4 * first_level : 4 * (first_level + count)]
    low_ref = low_ref.at[4 * first_level : 4 * (first_level + count)]
    for part in range(2):
        for unit in range(per):
            for core in range(fold):
                total = None
                for band in range(core, bands, fold):
                    begin = (band * 2 + part) * per + unit
                    value = recv_ref[pl.ds(begin, apertures, stride=bands * 2 * per), :]
                    total = value if total is None else total + value
                if fold == 1:
                    place = pl.ds(part * rows + unit * apertures, apertures)
                else:
                    place = pl.ds(part * rows + unit * fold + core, apertures, stride=bands)
                image_ref[0, place, :] = total
    for level in range(count):
        source, target = image_ref.at[level % 2], image_ref.at[(level + 1) % 2]
        result = level_step(level, half, source, (cos_ref, sin_ref), high_ref, low_ref)
        for parity in range(2):
            for part in range(2):
                target[pl.ds(part * rows + parity * half, half), :] = result[parity][part]
    last = image_ref.at[count % 2]
    power = last[0:rows, :] ** 2 + last[rows : 2 * rows, :] ** 2
    image_ref[(count + 1) % 2, 0:rows, :] = power
    edge = 8
    for part in range(2):
        pad_ref[part, 0:edge, :] = jnp.zeros((edge, LANES), jnp.float32)
        pad_ref[part, edge + rows :, :] = jnp.zeros((edge, LANES), jnp.float32)
    bits = rows.bit_length() - 1
    for row in range(rows):
        from_row = bit_reversed(row, bits)
        pad_ref[0, edge + row : edge + row + 1, :] = image_ref[
            (count + 1) % 2, from_row : from_row + 1, :
        ]
    power = pad_ref[0, edge : edge + rows, :]
    pad_ref[1, edge : edge + rows, :] = power * power
    sums = [
        box([pad_ref[part, edge + off : edge + off + rows, :] for off in range(-2, 3)])
        for part in range(2)
    ]
    shape = (rows, LANES)
    cells = near_count(iota(shape, 0), rows) * near_count(iota(shape, 1), LANES)
    cells = cells.astype(jnp.float32)
    mean, square = sums[0] / cells, sums[1] / cells
    gain = (square - mean * mean) / (square - 0.75 * mean * mean + 0.001)
    out_ref[...] = mean + gain * (power - mean)


def body(raw_echoes, pulse_order, matched, offsets, fraction, tilt_angle):
    bands, apertures = lax.axis_size("band"), lax.axis_size("aperture")
    devices = bands * apertures
    pulses, _, freq = raw_echoes.shape
    group = pulse_order.shape[-1]
    levels = tilt_angle.shape[0]
    tiles = freq // LANES
    fold = 2 if group == devices and bands % 2 == 0 else 1
    held = bands // fold
    rows = group * held
    local = (rows if fold == 1 else group).bit_length() - 1
    rest = levels - local
    inner = local - (devices.bit_length() - 1)
    per = rows // devices
    f32, bf16 = jnp.float32, jnp.bfloat16
    shape_of = jax.ShapeDtypeStruct
    vmem = pl.BlockSpec(memory_space=VMEM)
    params = pltpu.CompilerParams(vmem_limit_bytes=16 * 2**20)
    order = pulse_order.reshape(1, group)
    orders = [order]
    for apart in range(fold, bands, fold):
        orders.append(lax.ppermute(order, "band", [(n, n ^ apart) for n in range(bands)]))
    views = (
        raw_echoes.reshape(pulses, 2, tiles, LANES).transpose(0, 2, 1, 3),
        matched,
        offsets.transpose(1, 2, 3, 0),
        fraction.transpose(1, 2, 0),
        tilt_angle.transpose(1, 0),
        order,
    )
    views = [pltpu.with_memory_space_constraint(view, pltpu.HBM) for view in views]
    compress = pl.pallas_call(
        functools.partial(compress_kernel, matched.shape[1], local, fold),
        out_shape=[shape_of((2, rows, R), f32)] * fold
        + [
            shape_of((4 * levels, 8, LANES), f32),
            shape_of((2, 4 * levels, 8, LANES), f32),
            shape_of((8, LANES), f32),
            shape_of(order.shape, order.dtype),
        ],
        in_specs=[pl.BlockSpec(memory_space=pltpu.HBM)] * 6,
        out_specs=[vmem] * (4 + fold),
        scratch_shapes=[
            VMEM((tiles, 2 * R, LANES), bf16),
            VMEM((tiles, pulses, 2, LANES), bf16),
            VMEM((tiles, 2 * pulses, LANES), bf16),
            VMEM((2, 2 * pulses, R), f32),
            VMEM(matched.shape, f32),
            SMEM(views[2].shape, jnp.int32),
            SMEM(views[3].shape, f32),
            SMEM(views[4].shape, f32),
            pltpu.SemaphoreType.DMA((tiles,)),
            pltpu.SemaphoreType.DMA((tiles,)),
            pltpu.SemaphoreType.DMA((5,)),
        ],
        cost_estimate=pl.CostEstimate(
            flops=8 * pulses * freq * R, bytes_accessed=4 * pulses * freq, transcendentals=0
        ),
        compiler_params=params,
        name="compress",
    )
    *shares, starts, edges, angles, orders[0] = compress(*views)
    for side in range(1, fold):
        pairs = [(n, n ^ side) for n in range(bands)]
        shares[side] = lax.ppermute(shares[side], "band", pairs)
    final_rows = group
    matrices = pl.pallas_call(
        functools.partial(matrix_kernel, local, inner),
        out_shape=[
            shape_of((4 * levels, R, R), bf16),
            shape_of((4 * levels, R, R), bf16),
            shape_of((rows // 2, LANES), f32),
            shape_of((rows // 2, LANES), f32),
            shape_of((final_rows // 2, LANES), f32),
            shape_of((final_rows // 2, LANES), f32),
        ],
        in_specs=[vmem] * 3,
        out_specs=[vmem] * 6,
        scratch_shapes=[VMEM((R // 8, 8, LANES), f32)],
        cost_estimate=pl.CostEstimate(
            flops=400 * levels * R * R, bytes_accessed=16 * levels * R * R, transcendentals=0
        ),
        compiler_params=params,
        name="matrices",
    )
    high, low, cos_1, sin_1, cos_2, sin_2 = matrices(starts, edges, angles)
    sent = pl.pallas_call(
        functools.partial(local_kernel, local, fold),
        out_shape=shape_of((devices * 2 * per, R), f32),
        in_specs=[vmem] * (held + fold + 4),
        out_specs=vmem,
        scratch_shapes=[VMEM((2, 2 * rows, R), f32)],
        compiler_params=params,
        name="levels",
    )(*orders, *shares, high, low, cos_1, sin_1)
    received = lax.all_to_all(
        sent.reshape(devices, 2 * per, R), ("aperture", "band"), 0, 0, tiled=True
    ).reshape(devices * 2 * per, R)
    return pl.pallas_call(
        functools.partial(final_kernel, local, rest, fold),
        out_shape=shape_of((final_rows, R), f32),
        in_specs=[vmem] * 5,
        out_specs=vmem,
        scratch_shapes=[VMEM((2, 2 * final_rows, R), f32), VMEM((2, final_rows + 16, R), f32)],
        compiler_params=params,
        name="finish",
    )(received, high, low, cos_2, sin_2)


def solution(mesh):
    in_specs = (P("aperture", None, "band"), P("aperture", "band", None), P(), P(), P(), P())
    out_specs = P(("band", "aperture"), None)

    return jax.shard_map(body, mesh=mesh, in_specs=in_specs, out_specs=out_specs, check_vma=False)
```

```python
import functools
import math

import jax
import jax.numpy as jnp
from jax import lax
from jax.experimental import pallas as pl
from jax.experimental.pallas import tpu as pltpu
from jax.sharding import PartitionSpec as P

R = 128
SHIFT = 8
LANES = 128
VMEM = pltpu.VMEM
SMEM = pltpu.SMEM


def iota(shape, axis):
    return lax.broadcasted_iota(jnp.int32, shape, axis)


def bit_reversed(value, bits):
    result = value & 0
    for bit in range(bits):
        result = result | (((value >> bit) & 1) << (bits - 1 - bit))
    return result


def halves_of(value):
    high = value.astype(jnp.bfloat16)
    low = (value - high.astype(jnp.float32)).astype(jnp.bfloat16)
    return high, low


def cmul(first, second):
    return (
        first[0] * second[0] - first[1] * second[1],
        first[0] * second[1] + first[1] * second[0],
    )


def unit_rows(total_freq, start, chunks):
    turn = 2.0 * math.pi / total_freq
    rows = -(-chunks // 8) * 8
    f_index = start + iota((rows, LANES), 0) * LANES + iota((rows, LANES), 1)
    angle = f_index.astype(jnp.float32) * turn
    rows = (jnp.cos(angle), jnp.sin(angle))
    sub = iota((8, LANES), 0)
    result = []
    for chunk in range(chunks):
        power = [jnp.broadcast_to(part[chunk : chunk + 1, :], (8, LANES)) for part in rows]
        low = None
        for bit in range(3):
            chosen = (sub >> bit) & 1 == 1
            factor = (jnp.where(chosen, power[0], 1.0), jnp.where(chosen, power[1], 0.0))
            low = factor if low is None else cmul(low, factor)
            power = cmul(power, power)
        result.append((low, power))
    return result


def make_table(total_freq, start, units, matched_ref, table_ref, first):
    scale = 1.0 / math.sqrt(total_freq)
    for chunk, (low, power) in enumerate(units):
        lanes = pl.ds(pl.multiple_of(start + chunk * LANES, LANES), LANES)
        spec = matched_ref[:, lanes] * scale
        low = cmul([jnp.broadcast_to(spec[n : n + 1, :], (8, LANES)) for n in range(2)], low)
        block = [jnp.concatenate(parts, axis=0) for parts in zip(low, cmul(low, power))]
        power = cmul(power, power)
        power = [jnp.concatenate([part, part], axis=0) for part in power]
        for begin in range(0, R, 16):
            table_ref[first + chunk, begin : begin + 16, :] = block[0].astype(jnp.bfloat16)
            table_ref[first + chunk, R + begin : R + begin + 16, :] = block[1].astype(jnp.bfloat16)
            if begin + 16 < R:
                block = cmul(block, power)


def edge_bands():
    lane = iota((8, LANES), 1)
    period = 4 * SHIFT
    result = []
    for begin in range(0, R, 8):
        first = begin - SHIFT - 4
        result.append(jnp.where((lane >= first) & (lane < first + period), 1.0, 0.0))
    return result


def build_starts(levels, offsets_ref, fraction_ref, start_ref, edge_ref):
    period = 4 * SHIFT
    lane, row = iota((8, LANES), 1), iota((8, LANES), 0)
    near_tap = lane & (period - 1)
    tap = jnp.where(near_tap < period // 2, -near_tap, period - near_tap).astype(jnp.float32)
    bands = edge_bands()
    entries = [(n, c, p) for n in range(levels) for c in range(2) for p in range(2)]
    for block in range(0, len(entries), 8):
        here = entries[block : block + 8]
        shift = jnp.zeros((8, LANES), jnp.float32)
        for sub, (level, child, parity) in enumerate(here):
            shift = jnp.where(row == sub, fraction_ref[child, parity, level], shift)
        dist = tap - shift
        turn = math.pi * dist
        near = jnp.abs(dist) < 1e-12
        sinc = jnp.where(near, 1.0, jnp.sin(turn) / jnp.where(near, 1.0, turn))
        taper = sinc * jnp.exp(-((dist / 2.5) ** 2))
        taper = jnp.where(jnp.abs(dist) <= 4.0, taper, 0.0)
        for sub, (level, child, parity) in enumerate(here):
            moved = offsets_ref[child, parity, 0, level] - SHIFT
            one = jnp.broadcast_to(taper[sub : sub + 1, :], (8, LANES))
            one = pltpu.roll(one, (LANES - moved) & (LANES - 1), 1)
            start_ref[block + sub] = pltpu.roll(one, 0, 1, stride=1, stride_axis=0)
            edge_ref[0, block + sub] = jnp.where(row >= moved, bands[0], 0.0)
            edge_ref[1, block + sub] = jnp.where(row < moved + 8, bands[-1], 0.0)


def build_angles(first_level, count, tilt_ref):
    lane = iota((1, LANES), 1)
    angle = jnp.zeros((1, LANES), jnp.float32)
    for level in range(count):
        for child in range(2):
            angle = jnp.where(
                (lane >> 1) == 2 * level + child, tilt_ref[child, first_level + level], angle
            )
    return angle


def build_matrices(start_ref, edge_ref, band_ref, high_ref, low_ref):
    period = 4 * SHIFT
    for tile, band in enumerate(edge_bands()):
        band_ref[tile] = band
    last = R // 8 - 1
    for entry in range(start_ref.shape[0]):
        one = start_ref[entry]
        turned = [one] + [pltpu.roll(one, begin, 1) for begin in range(8, period, 8)]
        halves = []
        for value in turned:
            high = value.astype(jnp.bfloat16).astype(jnp.float32)
            halves.append((high, value - high))
        for begin in range(0, R, 16):
            for part, ref in enumerate((high_ref, low_ref)):
                tiles = []
                for tile in (begin // 8, begin // 8 + 1):
                    if tile in (0, last):
                        keep = edge_ref[tile // last, entry]
                    else:
                        keep = band_ref[tile]
                    tiles.append(halves[tile % len(halves)][part] * keep)
                ref[entry, begin : begin + 16, :] = jnp.concatenate(tiles, 0).astype(jnp.bfloat16)


def phase_tables(first_level, count, inner_bits, tile, angle, cos_ref, sin_ref):
    half = cos_ref.shape[0]
    bits = half.bit_length() - 1
    lane = iota((1, LANES), 1)
    step = jnp.ones((1, LANES), jnp.float32)
    mask = jnp.zeros((1, LANES), jnp.int32)
    tile_start = jnp.zeros((1, LANES), jnp.int32)
    for level in range(count):
        width = inner_bits + level
        here = (lane >> 2) == level
        step = jnp.where(here, 2.0 ** -(first_level + level), step)
        mask = jnp.where(here, 2**width - 1, mask)
        tile_start = jnp.where(here, tile * 2**width, tile_start)
    norm = 1.0 / math.sqrt(2.0)
    beam = tile_start + (bit_reversed(iota((8, LANES), 0), bits) & mask)
    j_index = (2 * beam + (lane & 1)).astype(jnp.float32)
    phi = angle * ((j_index + 0.5) * step - 1.0)
    inner = (jnp.cos(phi) * norm, jnp.sin(phi) * norm)
    groups = half // 8
    shape = (-(-groups // 8) * 8, LANES)
    beam = bit_reversed(iota(shape, 0) << 3, bits) & mask
    phi = angle * ((2 * beam).astype(jnp.float32) * step)
    outer = (jnp.cos(phi), jnp.sin(phi))
    for group in range(groups):
        co, si = cmul(inner, [part[group : group + 1, :] for part in outer])
        cos_ref[8 * group : 8 * group + 8, :] = co
        sin_ref[8 * group : 8 * group + 8, :] = si


def tables_kernel(total_freq, local, inner, fold, echo_hbm, matched_hbm, offsets_hbm, fraction_hbm,
                  tilt_hbm, order_hbm, echo_ref, order_ref, table_ref, high_ref, low_ref,
                  cos_ref, sin_ref, cos2_ref, sin2_ref, start_ref, edge_ref, band_ref, angle_ref,
                  matched_ref, offsets_ref, fraction_ref, tilt_ref, sems):
    pairs = (
        (matched_hbm, matched_ref),
        (offsets_hbm, offsets_ref),
        (fraction_hbm, fraction_ref),
        (tilt_hbm, tilt_ref),
        (order_hbm, order_ref),
        (echo_hbm, echo_ref),
    )
    copies = [pltpu.make_async_copy(*pair, sems.at[n]) for n, pair in enumerate(pairs)]
    for copy in copies:
        copy.start()
    tiles = echo_ref.shape[1]
    freq = tiles * LANES
    bands, apertures = lax.axis_size("band"), lax.axis_size("aperture")
    band = lax.axis_index("band")
    levels = start_ref.shape[0] // 4
    firsts = [(band ^ side) * freq for side in range(fold)]
    units = [unit_rows(total_freq, first, tiles) for first in firsts]
    copies[0].wait()
    for side in range(fold):
        make_table(total_freq, firsts[side], units[side], matched_ref, table_ref, side * tiles)
    for copy in copies[1:4]:
        copy.wait()
    build_starts(levels, offsets_ref, fraction_ref, start_ref, edge_ref)
    angle_ref[0:1, :] = build_angles(0, local, tilt_ref)
    angle_ref[1:2, :] = build_angles(local, levels - local, tilt_ref)
    build_matrices(start_ref, edge_ref, band_ref, high_ref, low_ref)
    phase_tables(0, local, 0, 0, angle_ref[0:1, :], cos_ref, sin_ref)
    place = lax.axis_index("aperture") * bands + band
    tile = bit_reversed(place, (bands * apertures).bit_length() - 1)
    phase_tables(local, levels - local, inner, tile, angle_ref[1:2, :], cos2_ref, sin2_ref)
    for copy in copies[4:]:
        copy.wait()


def level_step(level, half, source, tables, high_ref, low_ref):
    cos_ref, sin_ref = tables
    products = []
    for child in range(2):
        held = source[pl.ds(child, 2 * half, stride=2), :]
        high, low = halves_of(held)
        at = 4 * level + 2 * child
        m_high, m_low = (
            jnp.concatenate([ref[at], ref[at + 1]], axis=1) for ref in (high_ref, low_ref)
        )
        dot = functools.partial(jnp.dot, preferred_element_type=jnp.float32)
        both = jnp.concatenate([high, low], axis=1)
        m_both = jnp.concatenate([m_high, m_high], axis=0)
        products.append(dot(both, m_both) + dot(high, m_low))
    result = []
    for parity in range(2):
        re = im = None
        for child in range(2):
            entry = 4 * level + 2 * child + parity
            co = cos_ref[:, entry : entry + 1]
            si = sin_ref[:, entry : entry + 1]
            p_re = products[child][0:half, parity * R : (parity + 1) * R]
            p_im = products[child][half:, parity * R : (parity + 1) * R]
            r_new = p_re * co - p_im * si
            i_new = p_re * si + p_im * co
            re = r_new if re is None else re + r_new
            im = i_new if im is None else im + i_new
        result.append((re, im))
    return result


def product_kernel(fold, *refs):
    bands = lax.axis_size("band")
    echoes, (table_ref, prof_ref, sum_ref) = refs[:fold], refs[fold:]
    pulses, tiles = echoes[0].shape[:2]
    group = pulses // bands
    held = bands // fold
    core = lax.axis_index("band") & (fold - 1)
    pieces = []
    for echo_ref in echoes:
        for n in range(tiles):
            members = [
                echo_ref[pl.ds((member * fold + core) * group, group), n].reshape(2 * group, LANES)
                for member in range(held)
            ]
            pieces.append(jnp.concatenate(members, axis=0))
    table = jnp.concatenate([table_ref[n] for n in range(fold * tiles)], axis=1)
    sums = lax.dot_general(
        jnp.concatenate(pieces, axis=1),
        table,
        (((1,), (1,)), ((), ())),
        preferred_element_type=jnp.float32,
    )
    sum_ref[0] = sums[:, 0:R]
    sum_ref[1] = sums[:, R:]
    rows = group * held
    even, odd = pl.ds(0, rows, stride=2), pl.ds(1, rows, stride=2)
    values = (sum_ref[0, even, :] - sum_ref[1, odd, :], sum_ref[1, even, :] + sum_ref[0, odd, :])
    for part, value in enumerate(values):
        high, low = halves_of(value)
        prof_ref[part, 0:rows, :] = high
        prof_ref[part, rows:, :] = low


def local_kernel(count, fold, *refs):
    bands = lax.axis_size("band")
    devices = bands * lax.axis_size("aperture")
    held = bands // fold
    orders, refs = refs[:held], refs[held:]
    prof_ref, high_ref, low_ref, cos_ref, sin_ref, out_ref, image_ref = refs
    rows = prof_ref.shape[1] // 2
    group = rows // held
    half = rows // 2
    me = lax.axis_index("band") // fold
    for apart in range(held):
        start = pl.multiple_of((me ^ apart) * group, group)
        chosen = iota((group, group), 0) == jnp.broadcast_to(orders[apart][...], (group, group))
        chosen = jnp.where(chosen, 1.0, 0.0).astype(jnp.bfloat16)
        twice = jnp.concatenate([chosen, chosen], axis=0)
        parts = [
            jnp.concatenate(
                [prof_ref[part, pl.ds(side + start, group), :] for side in (0, rows)], axis=0
            )
            for part in range(2)
        ]
        moved = lax.dot_general(
            twice,
            jnp.concatenate(parts, axis=1),
            (((0,), (0,)), ((), ())),
            preferred_element_type=jnp.float32,
        )
        image_ref[0, pl.ds(start, group), :] = moved[:, 0:R]
        image_ref[0, pl.ds(rows + start, group), :] = moved[:, R:]
    for level in range(count):
        source, target = image_ref.at[level % 2], image_ref.at[(level + 1) % 2]
        result = level_step(level, half, source, (cos_ref, sin_ref), high_ref, low_ref)
        for parity in range(2):
            for part in range(2):
                target[pl.ds(part * rows + parity * half, half), :] = result[parity][part]
    last = image_ref.at[count % 2]
    per = rows // devices
    for part in range(2):
        for unit in range(per):
            if fold == 1:
                value = last[pl.ds(part * rows + unit * devices, devices), :]
            else:
                value = last[pl.ds(part * rows + unit, devices, stride=per), :]
            out_ref[pl.ds(part * per + unit, devices, stride=2 * per), :] = value


def box(rows):
    total = rows[0]
    for row in rows[1:]:
        total = total + row
    lane = iota(total.shape, 1)
    summed = total
    for off in (1, 2):
        right = pltpu.roll(total, off, 1)
        left = pltpu.roll(total, LANES - off, 1)
        summed = summed + jnp.where(lane >= off, right, 0.0)
        summed = summed + jnp.where(lane < LANES - off, left, 0.0)
    return summed


def near_count(position, size):
    return jnp.minimum(position, 2) + jnp.minimum(size - 1 - position, 2) + 1


def final_kernel(first_level, count, fold, recv_ref, high_ref, low_ref, cos_ref, sin_ref, out_ref,
                 image_ref, pad_ref):
    bands, apertures = lax.axis_size("band"), lax.axis_size("aperture")
    rows = out_ref.shape[0]
    half = rows // 2
    per = recv_ref.shape[0] // (2 * bands * apertures)
    high_ref = high_ref.at[4 * first_level : 4 * (first_level + count)]
    low_ref = low_ref.at[4 * first_level : 4 * (first_level + count)]
    for part in range(2):
        for unit in range(per):
            for core in range(fold):
                total = None
                for band in range(core, bands, fold):
                    begin = (band * 2 + part) * per + unit
                    value = recv_ref[pl.ds(begin, apertures, stride=bands * 2 * per), :]
                    total = value if total is None else total + value
                if fold == 1:
                    place = pl.ds(part * rows + unit * apertures, apertures)
                else:
                    place = pl.ds(part * rows + unit * fold + core, apertures, stride=bands)
                image_ref[0, place, :] = total
    for level in range(count):
        source, target = image_ref.at[level % 2], image_ref.at[(level + 1) % 2]
        result = level_step(level, half, source, (cos_ref, sin_ref), high_ref, low_ref)
        for parity in range(2):
            for part in range(2):
                target[pl.ds(part * rows + parity * half, half), :] = result[parity][part]
    last = image_ref.at[count % 2]
    power = last[0:rows, :] ** 2 + last[rows : 2 * rows, :] ** 2
    image_ref[(count + 1) % 2, 0:rows, :] = power
    edge = 8
    for part in range(2):
        pad_ref[part, 0:edge, :] = jnp.zeros((edge, LANES), jnp.float32)
        pad_ref[part, edge + rows :, :] = jnp.zeros((edge, LANES), jnp.float32)
    bits = rows.bit_length() - 1
    for row in range(rows):
        from_row = bit_reversed(row, bits)
        pad_ref[0, edge + row : edge + row + 1, :] = image_ref[
            (count + 1) % 2, from_row : from_row + 1, :
        ]
    power = pad_ref[0, edge : edge + rows, :]
    pad_ref[1, edge : edge + rows, :] = power * power
    sums = [
        box([pad_ref[part, edge + off : edge + off + rows, :] for off in range(-2, 3)])
        for part in range(2)
    ]
    shape = (rows, LANES)
    cells = near_count(iota(shape, 0), rows) * near_count(iota(shape, 1), LANES)
    cells = cells.astype(jnp.float32)
    mean, square = sums[0] / cells, sums[1] / cells
    gain = (square - mean * mean) / (square - 0.75 * mean * mean + 0.001)
    out_ref[...] = mean + gain * (power - mean)


def body(raw_echoes, pulse_order, matched, offsets, fraction, tilt_angle):
    bands, apertures = lax.axis_size("band"), lax.axis_size("aperture")
    devices = bands * apertures
    pulses, _, freq = raw_echoes.shape
    group = pulse_order.shape[-1]
    levels = tilt_angle.shape[0]
    tiles = freq // LANES
    fold = 2 if group == devices and bands % 2 == 0 else 1
    held = bands // fold
    rows = group * held
    local = (rows if fold == 1 else group).bit_length() - 1
    rest = levels - local
    inner = local - (devices.bit_length() - 1)
    per = rows // devices
    f32, bf16 = jnp.float32, jnp.bfloat16
    shape_of = jax.ShapeDtypeStruct
    vmem = pl.BlockSpec(memory_space=VMEM)
    params = pltpu.CompilerParams(vmem_limit_bytes=16 * 2**20)
    order = pulse_order.reshape(1, group)
    orders = [order]
    for apart in range(fold, bands, fold):
        orders.append(lax.ppermute(order, "band", [(n, n ^ apart) for n in range(bands)]))
    echo_parts = [raw_echoes]
    for side in range(1, fold):
        pairs = [(n, n ^ side) for n in range(bands)]
        echo_parts.append(lax.ppermute(raw_echoes, "band", pairs))
    echoes = [
        part.reshape(pulses, 2, tiles, LANES).transpose(0, 2, 1, 3) for part in echo_parts
    ]
    views = (
        echoes[0],
        matched,
        offsets.transpose(1, 2, 3, 0),
        fraction.transpose(1, 2, 0),
        tilt_angle.transpose(1, 0),
        order,
    )
    views = [pltpu.with_memory_space_constraint(view, pltpu.HBM) for view in views]
    tables = pl.pallas_call(
        functools.partial(tables_kernel, matched.shape[1], local, inner, fold),
        out_shape=[
            shape_of(echoes[0].shape, bf16),
            shape_of(order.shape, order.dtype),
            shape_of((fold * tiles, 2 * R, LANES), bf16),
            shape_of((4 * levels, R, R), bf16),
            shape_of((4 * levels, R, R), bf16),
            shape_of((rows // 2, LANES), f32),
            shape_of((rows // 2, LANES), f32),
            shape_of((group // 2, LANES), f32),
            shape_of((group // 2, LANES), f32),
        ],
        in_specs=[pl.BlockSpec(memory_space=pltpu.HBM)] * 6,
        out_specs=[vmem] * 9,
        scratch_shapes=[
            VMEM((4 * levels, 8, LANES), f32),
            VMEM((2, 4 * levels, 8, LANES), f32),
            VMEM((R // 8, 8, LANES), f32),
            VMEM((8, LANES), f32),
            VMEM(matched.shape, f32),
            SMEM(views[2].shape, jnp.int32),
            SMEM(views[3].shape, f32),
            SMEM(views[4].shape, f32),
            pltpu.SemaphoreType.DMA((6,)),
        ],
        cost_estimate=pl.CostEstimate(
            flops=400 * levels * R * R, bytes_accessed=16 * levels * R * R, transcendentals=0
        ),
        compiler_params=params,
        name="tables",
    )
    echoes[0], orders[0], table, high, low, cos_1, sin_1, cos_2, sin_2 = tables(*views)
    product = pl.pallas_call(
        functools.partial(product_kernel, fold),
        out_shape=shape_of((2, 2 * rows, R), bf16),
        in_specs=[vmem] * (fold + 1),
        out_specs=vmem,
        scratch_shapes=[VMEM((2, 2 * rows, R), f32)],
        cost_estimate=pl.CostEstimate(
            flops=8 * pulses * freq * R, bytes_accessed=4 * pulses * freq, transcendentals=0
        ),
        compiler_params=params,
        name="product",
    )
    prof = product(*echoes, table)
    sent = pl.pallas_call(
        functools.partial(local_kernel, local, fold),
        out_shape=shape_of((devices * 2 * per, R), f32),
        in_specs=[vmem] * (held + 5),
        out_specs=vmem,
        scratch_shapes=[VMEM((2, 2 * rows, R), f32)],
        compiler_params=params,
        name="levels",
    )(*orders, prof, high, low, cos_1, sin_1)
    received = lax.all_to_all(
        sent.reshape(devices, 2 * per, R), ("aperture", "band"), 0, 0, tiled=True
    ).reshape(devices * 2 * per, R)
    return pl.pallas_call(
        functools.partial(final_kernel, local, rest, fold),
        out_shape=shape_of((group, R), f32),
        in_specs=[vmem] * 5,
        out_specs=vmem,
        scratch_shapes=[VMEM((2, 2 * group, R), f32), VMEM((2, group + 16, R), f32)],
        compiler_params=params,
        name="finish",
    )(received, high, low, cos_2, sin_2)


def solution(mesh):
    in_specs = (P("aperture", None, "band"), P("aperture", "band", None), P(), P(), P(), P())
    out_specs = P(("band", "aperture"), None)

    return jax.shard_map(body, mesh=mesh, in_specs=in_specs, out_specs=out_specs, check_vma=False)
```

```python
import functools
import math

import jax
import jax.numpy as jnp
from jax import lax
from jax.experimental import pallas as pl
from jax.experimental.pallas import tpu as pltpu
from jax.sharding import PartitionSpec as P

R = 128
SHIFT = 8
LANES = 128
VMEM = pltpu.VMEM
SMEM = pltpu.SMEM


def iota(shape, axis):
    return lax.broadcasted_iota(jnp.int32, shape, axis)


def bit_reversed(value, bits):
    result = value & 0
    for bit in range(bits):
        result = result | (((value >> bit) & 1) << (bits - 1 - bit))
    return result


def halves_of(value):
    high = value.astype(jnp.bfloat16)
    low = (value - high.astype(jnp.float32)).astype(jnp.bfloat16)
    return high, low


def cmul(first, second):
    return (
        first[0] * second[0] - first[1] * second[1],
        first[0] * second[1] + first[1] * second[0],
    )


def unit_rows(total_freq, start, chunks):
    turn = 2.0 * math.pi / total_freq
    rows = -(-chunks // 8) * 8
    f_index = start + iota((rows, LANES), 0) * LANES + iota((rows, LANES), 1)
    angle = f_index.astype(jnp.float32) * turn
    rows = (jnp.cos(angle), jnp.sin(angle))
    sub = iota((8, LANES), 0)
    result = []
    for chunk in range(chunks):
        power = [jnp.broadcast_to(part[chunk : chunk + 1, :], (8, LANES)) for part in rows]
        low = None
        for bit in range(3):
            chosen = (sub >> bit) & 1 == 1
            factor = (jnp.where(chosen, power[0], 1.0), jnp.where(chosen, power[1], 0.0))
            low = factor if low is None else cmul(low, factor)
            power = cmul(power, power)
        result.append((low, power))
    return result


def make_table(total_freq, start, units, matched_ref, table_ref, first):
    scale = 1.0 / math.sqrt(total_freq)
    for chunk, (low, power) in enumerate(units):
        lanes = pl.ds(pl.multiple_of(start + chunk * LANES, LANES), LANES)
        spec = matched_ref[:, lanes] * scale
        low = cmul([jnp.broadcast_to(spec[n : n + 1, :], (8, LANES)) for n in range(2)], low)
        block = [jnp.concatenate(parts, axis=0) for parts in zip(low, cmul(low, power))]
        power = cmul(power, power)
        power = [jnp.concatenate([part, part], axis=0) for part in power]
        for begin in range(0, R, 16):
            table_ref[first + chunk, begin : begin + 16, :] = block[0].astype(jnp.bfloat16)
            table_ref[first + chunk, R + begin : R + begin + 16, :] = block[1].astype(jnp.bfloat16)
            if begin + 16 < R:
                block = cmul(block, power)


def edge_bands():
    lane = iota((8, LANES), 1)
    period = 4 * SHIFT
    result = []
    for begin in range(0, R, 8):
        first = begin - SHIFT - 4
        result.append(jnp.where((lane >= first) & (lane < first + period), 1.0, 0.0))
    return result


def build_starts(levels, offsets_ref, fraction_ref, start_ref, edge_ref):
    period = 4 * SHIFT
    lane, row = iota((8, LANES), 1), iota((8, LANES), 0)
    near_tap = lane & (period - 1)
    tap = jnp.where(near_tap < period // 2, -near_tap, period - near_tap).astype(jnp.float32)
    bands = edge_bands()
    entries = [(n, c, p) for n in range(levels) for c in range(2) for p in range(2)]
    for block in range(0, len(entries), 8):
        here = entries[block : block + 8]
        shift = jnp.zeros((8, LANES), jnp.float32)
        for sub, (level, child, parity) in enumerate(here):
            shift = jnp.where(row == sub, fraction_ref[child, parity, level], shift)
        dist = tap - shift
        turn = math.pi * dist
        near = jnp.abs(dist) < 1e-12
        sinc = jnp.where(near, 1.0, jnp.sin(turn) / jnp.where(near, 1.0, turn))
        taper = sinc * jnp.exp(-((dist / 2.5) ** 2))
        taper = jnp.where(jnp.abs(dist) <= 4.0, taper, 0.0)
        for sub, (level, child, parity) in enumerate(here):
            moved = offsets_ref[child, parity, 0, level] - SHIFT
            one = jnp.broadcast_to(taper[sub : sub + 1, :], (8, LANES))
            one = pltpu.roll(one, (LANES - moved) & (LANES - 1), 1)
            start_ref[block + sub] = pltpu.roll(one, 0, 1, stride=1, stride_axis=0)
            edge_ref[0, block + sub] = jnp.where(row >= moved, bands[0], 0.0)
            edge_ref[1, block + sub] = jnp.where(row < moved + 8, bands[-1], 0.0)


def build_angles(first_level, count, tilt_ref):
    lane = iota((1, LANES), 1)
    angle = jnp.zeros((1, LANES), jnp.float32)
    for level in range(count):
        for child in range(2):
            angle = jnp.where(
                (lane >> 1) == 2 * level + child, tilt_ref[child, first_level + level], angle
            )
    return angle


def build_matrices(start_ref, edge_ref, band_ref, high_ref, low_ref):
    period = 4 * SHIFT
    for tile, band in enumerate(edge_bands()):
        band_ref[tile] = band
    last = R // 8 - 1
    for entry in range(start_ref.shape[0]):
        one = start_ref[entry]
        turned = [one] + [pltpu.roll(one, begin, 1) for begin in range(8, period, 8)]
        halves = []
        for value in turned:
            high = value.astype(jnp.bfloat16).astype(jnp.float32)
            halves.append((high, value - high))
        for begin in range(0, R, 16):
            for part, ref in enumerate((high_ref, low_ref)):
                tiles = []
                for tile in (begin // 8, begin // 8 + 1):
                    if tile in (0, last):
                        keep = edge_ref[tile // last, entry]
                    else:
                        keep = band_ref[tile]
                    tiles.append(halves[tile % len(halves)][part] * keep)
                ref[entry, begin : begin + 16, :] = jnp.concatenate(tiles, 0).astype(jnp.bfloat16)


def phase_tables(first_level, count, inner_bits, tile, angle, cos_ref, sin_ref):
    half = cos_ref.shape[0]
    bits = half.bit_length() - 1
    lane = iota((1, LANES), 1)
    step = jnp.ones((1, LANES), jnp.float32)
    mask = jnp.zeros((1, LANES), jnp.int32)
    tile_start = jnp.zeros((1, LANES), jnp.int32)
    for level in range(count):
        width = inner_bits + level
        here = (lane >> 2) == level
        step = jnp.where(here, 2.0 ** -(first_level + level), step)
        mask = jnp.where(here, 2**width - 1, mask)
        tile_start = jnp.where(here, tile * 2**width, tile_start)
    norm = 1.0 / math.sqrt(2.0)
    beam = tile_start + (bit_reversed(iota((8, LANES), 0), bits) & mask)
    j_index = (2 * beam + (lane & 1)).astype(jnp.float32)
    phi = angle * ((j_index + 0.5) * step - 1.0)
    inner = (jnp.cos(phi) * norm, jnp.sin(phi) * norm)
    groups = half // 8
    shape = (-(-groups // 8) * 8, LANES)
    beam = bit_reversed(iota(shape, 0) << 3, bits) & mask
    phi = angle * ((2 * beam).astype(jnp.float32) * step)
    outer = (jnp.cos(phi), jnp.sin(phi))
    for group in range(groups):
        co, si = cmul(inner, [part[group : group + 1, :] for part in outer])
        cos_ref[8 * group : 8 * group + 8, :] = co
        sin_ref[8 * group : 8 * group + 8, :] = si


def tables_kernel(total_freq, local, inner, fold, echo_hbm, matched_hbm, offsets_hbm, fraction_hbm,
                  tilt_hbm, order_hbm, echo_ref, order_ref, table_ref, high_ref, low_ref,
                  cos_ref, sin_ref, cos2_ref, sin2_ref, start_ref, edge_ref, band_ref, angle_ref,
                  matched_ref, offsets_ref, fraction_ref, tilt_ref, sems):
    pairs = (
        (matched_hbm, matched_ref),
        (offsets_hbm, offsets_ref),
        (fraction_hbm, fraction_ref),
        (tilt_hbm, tilt_ref),
        (order_hbm, order_ref),
        (echo_hbm, echo_ref),
    )
    copies = [pltpu.make_async_copy(*pair, sems.at[n]) for n, pair in enumerate(pairs)]
    for copy in copies:
        copy.start()
    tiles = echo_ref.shape[1]
    freq = tiles * LANES
    bands, apertures = lax.axis_size("band"), lax.axis_size("aperture")
    band = lax.axis_index("band")
    levels = start_ref.shape[0] // 4
    firsts = [(band ^ side) * freq for side in range(fold)]
    units = [unit_rows(total_freq, first, tiles) for first in firsts]
    copies[0].wait()
    for side in range(fold):
        make_table(total_freq, firsts[side], units[side], matched_ref, table_ref, side * tiles)
    for copy in copies[1:4]:
        copy.wait()
    build_starts(levels, offsets_ref, fraction_ref, start_ref, edge_ref)
    angle_ref[0:1, :] = build_angles(0, local, tilt_ref)
    angle_ref[1:2, :] = build_angles(local, levels - local, tilt_ref)
    build_matrices(start_ref, edge_ref, band_ref, high_ref, low_ref)
    phase_tables(0, local, 0, 0, angle_ref[0:1, :], cos_ref, sin_ref)
    place = lax.axis_index("aperture") * bands + band
    tile = bit_reversed(place, (bands * apertures).bit_length() - 1)
    phase_tables(local, levels - local, inner, tile, angle_ref[1:2, :], cos2_ref, sin2_ref)
    for copy in copies[4:]:
        copy.wait()


def interpolated(held, at, high_ref, low_ref):
    high, low = halves_of(held)
    m_high, m_low = (
        jnp.concatenate([ref[at], ref[at + 1]], axis=1) for ref in (high_ref, low_ref)
    )
    dot = functools.partial(jnp.dot, preferred_element_type=jnp.float32)
    both = jnp.concatenate([high, low], axis=1)
    return dot(both, jnp.concatenate([m_high, m_high], axis=0)) + dot(high, m_low)


def children_of(source, half):
    return [source[pl.ds(child, 2 * half, stride=2), :] for child in range(2)]


def level_step(level, half, children, tables, high_ref, low_ref):
    cos_ref, sin_ref = tables
    products = [
        interpolated(held, 4 * level + 2 * child, high_ref, low_ref)
        for child, held in enumerate(children)
    ]
    result = []
    for parity in range(2):
        re = im = None
        for child in range(2):
            entry = 4 * level + 2 * child + parity
            co = cos_ref[:, entry : entry + 1]
            si = sin_ref[:, entry : entry + 1]
            p_re = products[child][0:half, parity * R : (parity + 1) * R]
            p_im = products[child][half:, parity * R : (parity + 1) * R]
            r_new = p_re * co - p_im * si
            i_new = p_re * si + p_im * co
            re = r_new if re is None else re + r_new
            im = i_new if im is None else im + i_new
        result.append((re, im))
    return result


def product_kernel(fold, *refs):
    bands = lax.axis_size("band")
    echoes, refs = refs[:fold], refs[fold:]
    table_ref, high_ref, low_ref, cos_ref, sin_ref, prof_ref, sum_ref = refs
    pulses, tiles = echoes[0].shape[:2]
    group = pulses // bands
    held = bands // fold
    core = lax.axis_index("band") & (fold - 1)
    pieces = []
    for echo_ref in echoes:
        for n in range(tiles):
            members = [
                echo_ref[pl.ds((member * fold + core) * group, group), n].reshape(2 * group, LANES)
                for member in range(held)
            ]
            pieces.append(jnp.concatenate(members, axis=0))
    table = jnp.concatenate([table_ref[n] for n in range(fold * tiles)], axis=1)
    sums = lax.dot_general(
        jnp.concatenate(pieces, axis=1),
        table,
        (((1,), (1,)), ((), ())),
        preferred_element_type=jnp.float32,
    )
    sum_ref[0] = sums[:, 0:R]
    sum_ref[1] = sums[:, R:]
    rows = group * held
    even, odd = pl.ds(0, rows, stride=2), pl.ds(1, rows, stride=2)
    values = (sum_ref[0, even, :] - sum_ref[1, odd, :], sum_ref[1, even, :] + sum_ref[0, odd, :])
    both = jnp.concatenate(values, axis=0)
    for child in range(2):
        result = interpolated(both, 2 * child, high_ref, low_ref)
        for parity in range(2):
            entry = 2 * child + parity
            phase = (cos_ref[0:1, entry : entry + 1], sin_ref[0:1, entry : entry + 1])
            column = slice(parity * R, (parity + 1) * R)
            turned = cmul((result[0:rows, column], result[rows:, column]), phase)
            for part, value in enumerate(turned):
                for side, half in enumerate(halves_of(value)):
                    at = (2 * side + child) * group
                    for member in range(held):
                        prof_ref[parity, part, member, at : at + group, :] = half[
                            member * group : (member + 1) * group
                        ]


def local_kernel(count, fold, *refs):
    bands = lax.axis_size("band")
    devices = bands * lax.axis_size("aperture")
    held = bands // fold
    orders, refs = refs[:held], refs[held:]
    prof_ref, high_ref, low_ref, cos_ref, sin_ref, out_ref, image_ref, pick_ref = refs
    group = prof_ref.shape[3] // 4
    rows = group * held
    half = rows // 2
    me = lax.axis_index("band") // fold
    for apart in range(held):
        member = me ^ apart
        start = pl.multiple_of(member * group, group)
        match = iota((group, group), 0) == jnp.broadcast_to(orders[apart][...], (group, group))
        lane = iota((group, group), 1)
        chosen = [jnp.where(match & (lane & 1 == child), 1.0, 0.0) for child in range(2)]
        chosen = jnp.concatenate(chosen + chosen, axis=0).astype(jnp.bfloat16)
        for parity in range(2):
            moved = lax.dot_general(
                chosen,
                jnp.concatenate([prof_ref[parity, part, member] for part in range(2)], axis=1),
                (((0,), (0,)), ((), ())),
                preferred_element_type=jnp.float32,
            )
            for part in range(2):
                pick_ref[parity, part, pl.ds(start, group), :] = moved[:, part * R : (part + 1) * R]
    for level in range(1, count):
        source, target = image_ref.at[level % 2], image_ref.at[(level + 1) % 2]
        if level == 1:
            children = []
            for child in range(0, 4, 2):
                parts = [
                    pick_ref[parity, part, pl.ds(child, rows // 4, stride=4), :]
                    + pick_ref[parity, part, pl.ds(child + 1, rows // 4, stride=4), :]
                    for part in range(2)
                    for parity in range(2)
                ]
                children.append(jnp.concatenate(parts, axis=0))
        else:
            children = children_of(source, half)
        result = level_step(level, half, children, (cos_ref, sin_ref), high_ref, low_ref)
        for parity in range(2):
            for part in range(2):
                target[pl.ds(part * rows + parity * half, half), :] = result[parity][part]
    last = image_ref.at[count % 2]
    per = rows // devices
    for part in range(2):
        for unit in range(per):
            if fold == 1:
                value = last[pl.ds(part * rows + unit * devices, devices), :]
            else:
                value = last[pl.ds(part * rows + unit, devices, stride=per), :]
            out_ref[pl.ds(part * per + unit, devices, stride=2 * per), :] = value


def box(rows):
    total = rows[0]
    for row in rows[1:]:
        total = total + row
    lane = iota(total.shape, 1)
    summed = total
    for off in (1, 2):
        right = pltpu.roll(total, off, 1)
        left = pltpu.roll(total, LANES - off, 1)
        summed = summed + jnp.where(lane >= off, right, 0.0)
        summed = summed + jnp.where(lane < LANES - off, left, 0.0)
    return summed


def near_count(position, size):
    return jnp.minimum(position, 2) + jnp.minimum(size - 1 - position, 2) + 1


def final_kernel(first_level, count, fold, recv_ref, high_ref, low_ref, cos_ref, sin_ref, out_ref,
                 image_ref, pad_ref):
    bands, apertures = lax.axis_size("band"), lax.axis_size("aperture")
    rows = out_ref.shape[0]
    half = rows // 2
    per = recv_ref.shape[0] // (2 * bands * apertures)
    high_ref = high_ref.at[4 * first_level : 4 * (first_level + count)]
    low_ref = low_ref.at[4 * first_level : 4 * (first_level + count)]
    for part in range(2):
        for unit in range(per):
            for core in range(fold):
                total = None
                for band in range(core, bands, fold):
                    begin = (band * 2 + part) * per + unit
                    value = recv_ref[pl.ds(begin, apertures, stride=bands * 2 * per), :]
                    total = value if total is None else total + value
                if fold == 1:
                    place = pl.ds(part * rows + unit * apertures, apertures)
                else:
                    place = pl.ds(part * rows + unit * fold + core, apertures, stride=bands)
                image_ref[0, place, :] = total
    for level in range(count):
        source, target = image_ref.at[level % 2], image_ref.at[(level + 1) % 2]
        children = children_of(source, half)
        result = level_step(level, half, children, (cos_ref, sin_ref), high_ref, low_ref)
        for parity in range(2):
            for part in range(2):
                target[pl.ds(part * rows + parity * half, half), :] = result[parity][part]
    last = image_ref.at[count % 2]
    power = last[0:rows, :] ** 2 + last[rows : 2 * rows, :] ** 2
    image_ref[(count + 1) % 2, 0:rows, :] = power
    edge = 8
    for part in range(2):
        pad_ref[part, 0:edge, :] = jnp.zeros((edge, LANES), jnp.float32)
        pad_ref[part, edge + rows :, :] = jnp.zeros((edge, LANES), jnp.float32)
    bits = rows.bit_length() - 1
    for row in range(rows):
        from_row = bit_reversed(row, bits)
        pad_ref[0, edge + row : edge + row + 1, :] = image_ref[
            (count + 1) % 2, from_row : from_row + 1, :
        ]
    power = pad_ref[0, edge : edge + rows, :]
    pad_ref[1, edge : edge + rows, :] = power * power
    sums = [
        box([pad_ref[part, edge + off : edge + off + rows, :] for off in range(-2, 3)])
        for part in range(2)
    ]
    shape = (rows, LANES)
    cells = near_count(iota(shape, 0), rows) * near_count(iota(shape, 1), LANES)
    cells = cells.astype(jnp.float32)
    mean, square = sums[0] / cells, sums[1] / cells
    gain = (square - mean * mean) / (square - 0.75 * mean * mean + 0.001)
    out_ref[...] = mean + gain * (power - mean)


def body(raw_echoes, pulse_order, matched, offsets, fraction, tilt_angle):
    bands, apertures = lax.axis_size("band"), lax.axis_size("aperture")
    devices = bands * apertures
    pulses, _, freq = raw_echoes.shape
    group = pulse_order.shape[-1]
    levels = tilt_angle.shape[0]
    tiles = freq // LANES
    fold = 2 if group == devices and bands % 2 == 0 else 1
    held = bands // fold
    rows = group * held
    local = (rows if fold == 1 else group).bit_length() - 1
    rest = levels - local
    inner = local - (devices.bit_length() - 1)
    per = rows // devices
    f32, bf16 = jnp.float32, jnp.bfloat16
    shape_of = jax.ShapeDtypeStruct
    vmem = pl.BlockSpec(memory_space=VMEM)
    params = pltpu.CompilerParams(vmem_limit_bytes=16 * 2**20)
    order = pulse_order.reshape(1, group)
    orders = [order]
    for apart in range(fold, bands, fold):
        orders.append(lax.ppermute(order, "band", [(n, n ^ apart) for n in range(bands)]))
    echo_parts = [raw_echoes]
    for side in range(1, fold):
        pairs = [(n, n ^ side) for n in range(bands)]
        echo_parts.append(lax.ppermute(raw_echoes, "band", pairs))
    echoes = [
        part.reshape(pulses, 2, tiles, LANES).transpose(0, 2, 1, 3) for part in echo_parts
    ]
    views = (
        echoes[0],
        matched,
        offsets.transpose(1, 2, 3, 0),
        fraction.transpose(1, 2, 0),
        tilt_angle.transpose(1, 0),
        order,
    )
    views = [pltpu.with_memory_space_constraint(view, pltpu.HBM) for view in views]
    tables = pl.pallas_call(
        functools.partial(tables_kernel, matched.shape[1], local, inner, fold),
        out_shape=[
            shape_of(echoes[0].shape, bf16),
            shape_of(order.shape, order.dtype),
            shape_of((fold * tiles, 2 * R, LANES), bf16),
            shape_of((4 * levels, R, R), bf16),
            shape_of((4 * levels, R, R), bf16),
            shape_of((rows // 2, LANES), f32),
            shape_of((rows // 2, LANES), f32),
            shape_of((group // 2, LANES), f32),
            shape_of((group // 2, LANES), f32),
        ],
        in_specs=[pl.BlockSpec(memory_space=pltpu.HBM)] * 6,
        out_specs=[vmem] * 9,
        scratch_shapes=[
            VMEM((4 * levels, 8, LANES), f32),
            VMEM((2, 4 * levels, 8, LANES), f32),
            VMEM((R // 8, 8, LANES), f32),
            VMEM((8, LANES), f32),
            VMEM(matched.shape, f32),
            SMEM(views[2].shape, jnp.int32),
            SMEM(views[3].shape, f32),
            SMEM(views[4].shape, f32),
            pltpu.SemaphoreType.DMA((6,)),
        ],
        cost_estimate=pl.CostEstimate(
            flops=400 * levels * R * R, bytes_accessed=16 * levels * R * R, transcendentals=0
        ),
        compiler_params=params,
        name="tables",
    )
    echoes[0], orders[0], table, high, low, cos_1, sin_1, cos_2, sin_2 = tables(*views)
    product = pl.pallas_call(
        functools.partial(product_kernel, fold),
        out_shape=shape_of((2, 2, held, 4 * group, R), bf16),
        in_specs=[vmem] * (fold + 5),
        out_specs=vmem,
        scratch_shapes=[VMEM((2, 2 * rows, R), f32)],
        cost_estimate=pl.CostEstimate(
            flops=8 * pulses * freq * R, bytes_accessed=4 * pulses * freq, transcendentals=0
        ),
        compiler_params=params,
        name="product",
    )
    prof = product(*echoes, table, high, low, cos_1, sin_1)
    sent = pl.pallas_call(
        functools.partial(local_kernel, local, fold),
        out_shape=shape_of((devices * 2 * per, R), f32),
        in_specs=[vmem] * (held + 5),
        out_specs=vmem,
        scratch_shapes=[VMEM((2, 2 * rows, R), f32), VMEM((2, 2, rows, R), f32)],
        compiler_params=params,
        name="levels",
    )(*orders, prof, high, low, cos_1, sin_1)
    received = lax.all_to_all(
        sent.reshape(devices, 2 * per, R), ("aperture", "band"), 0, 0, tiled=True
    ).reshape(devices * 2 * per, R)
    return pl.pallas_call(
        functools.partial(final_kernel, local, rest, fold),
        out_shape=shape_of((group, R), f32),
        in_specs=[vmem] * 5,
        out_specs=vmem,
        scratch_shapes=[VMEM((2, 2 * group, R), f32), VMEM((2, group + 16, R), f32)],
        compiler_params=params,
        name="finish",
    )(received, high, low, cos_2, sin_2)


def solution(mesh):
    in_specs = (P("aperture", None, "band"), P("aperture", "band", None), P(), P(), P(), P())
    out_specs = P(("band", "aperture"), None)

    return jax.shard_map(body, mesh=mesh, in_specs=in_specs, out_specs=out_specs, check_vma=False)
```

```python
import functools
import math

import jax
import jax.numpy as jnp
from jax import lax
from jax.experimental import pallas as pl
from jax.experimental.pallas import tpu as pltpu
from jax.sharding import PartitionSpec as P

R = 128
SHIFT = 8
LANES = 128
VMEM = pltpu.VMEM
SMEM = pltpu.SMEM


def iota(shape, axis):
    return lax.broadcasted_iota(jnp.int32, shape, axis)


def bit_reversed(value, bits):
    result = value & 0
    for bit in range(bits):
        result = result | (((value >> bit) & 1) << (bits - 1 - bit))
    return result


def halves_of(value):
    high = value.astype(jnp.bfloat16)
    low = (value - high.astype(jnp.float32)).astype(jnp.bfloat16)
    return high, low


def cmul(first, second):
    return (
        first[0] * second[0] - first[1] * second[1],
        first[0] * second[1] + first[1] * second[0],
    )


def unit_rows(total_freq, start, chunks):
    turn = 2.0 * math.pi / total_freq
    rows = -(-chunks // 8) * 8
    f_index = start + iota((rows, LANES), 0) * LANES + iota((rows, LANES), 1)
    angle = f_index.astype(jnp.float32) * turn
    rows = (jnp.cos(angle), jnp.sin(angle))
    sub = iota((8, LANES), 0)
    result = []
    for chunk in range(chunks):
        power = [jnp.broadcast_to(part[chunk : chunk + 1, :], (8, LANES)) for part in rows]
        low = None
        for bit in range(3):
            chosen = (sub >> bit) & 1 == 1
            factor = (jnp.where(chosen, power[0], 1.0), jnp.where(chosen, power[1], 0.0))
            low = factor if low is None else cmul(low, factor)
            power = cmul(power, power)
        result.append((low, power))
    return result


def make_table(total_freq, start, units, matched_ref, table_ref, first):
    scale = 1.0 / math.sqrt(total_freq)
    for chunk, (low, power) in enumerate(units):
        lanes = pl.ds(pl.multiple_of(start + chunk * LANES, LANES), LANES)
        spec = matched_ref[:, lanes] * scale
        low = cmul([jnp.broadcast_to(spec[n : n + 1, :], (8, LANES)) for n in range(2)], low)
        block = [jnp.concatenate(parts, axis=0) for parts in zip(low, cmul(low, power))]
        power = cmul(power, power)
        power = [jnp.concatenate([part, part], axis=0) for part in power]
        for begin in range(0, R, 16):
            table_ref[first + chunk, begin : begin + 16, :] = block[0].astype(jnp.bfloat16)
            table_ref[first + chunk, R + begin : R + begin + 16, :] = block[1].astype(jnp.bfloat16)
            if begin + 16 < R:
                block = cmul(block, power)


def edge_bands():
    lane = iota((8, LANES), 1)
    period = 4 * SHIFT
    result = []
    for begin in range(0, R, 8):
        first = begin - SHIFT - 4
        result.append(jnp.where((lane >= first) & (lane < first + period), 1.0, 0.0))
    return result


def build_starts(levels, offsets_ref, fraction_ref, start_ref, edge_ref):
    period = 4 * SHIFT
    lane, row = iota((8, LANES), 1), iota((8, LANES), 0)
    near_tap = lane & (period - 1)
    tap = jnp.where(near_tap < period // 2, -near_tap, period - near_tap).astype(jnp.float32)
    bands = edge_bands()
    entries = [(n, c, p) for n in range(levels) for c in range(2) for p in range(2)]
    for block in range(0, len(entries), 8):
        here = entries[block : block + 8]
        shift = jnp.zeros((8, LANES), jnp.float32)
        for sub, (level, child, parity) in enumerate(here):
            shift = jnp.where(row == sub, fraction_ref[child, parity, level], shift)
        dist = tap - shift
        turn = math.pi * dist
        near = jnp.abs(dist) < 1e-12
        sinc = jnp.where(near, 1.0, jnp.sin(turn) / jnp.where(near, 1.0, turn))
        taper = sinc * jnp.exp(-((dist / 2.5) ** 2))
        taper = jnp.where(jnp.abs(dist) <= 4.0, taper, 0.0)
        for sub, (level, child, parity) in enumerate(here):
            moved = offsets_ref[child, parity, 0, level] - SHIFT
            one = jnp.broadcast_to(taper[sub : sub + 1, :], (8, LANES))
            one = pltpu.roll(one, (LANES - moved) & (LANES - 1), 1)
            start_ref[block + sub] = pltpu.roll(one, 0, 1, stride=1, stride_axis=0)
            edge_ref[0, block + sub] = jnp.where(row >= moved, bands[0], 0.0)
            edge_ref[1, block + sub] = jnp.where(row < moved + 8, bands[-1], 0.0)


def build_angles(first_level, count, tilt_ref):
    lane = iota((1, LANES), 1)
    angle = jnp.zeros((1, LANES), jnp.float32)
    for level in range(count):
        for child in range(2):
            angle = jnp.where(
                (lane >> 1) == 2 * level + child, tilt_ref[child, first_level + level], angle
            )
    return angle


def build_matrices(start_ref, edge_ref, band_ref, high_ref, low_ref):
    period = 4 * SHIFT
    for tile, band in enumerate(edge_bands()):
        band_ref[tile] = band
    last = R // 8 - 1
    for entry in range(start_ref.shape[0]):
        one = start_ref[entry]
        turned = [one] + [pltpu.roll(one, begin, 1) for begin in range(8, period, 8)]
        halves = []
        for value in turned:
            high = value.astype(jnp.bfloat16).astype(jnp.float32)
            halves.append((high, value - high))
        for begin in range(0, R, 16):
            for part, ref in enumerate((high_ref, low_ref)):
                tiles = []
                for tile in (begin // 8, begin // 8 + 1):
                    if tile in (0, last):
                        keep = edge_ref[tile // last, entry]
                    else:
                        keep = band_ref[tile]
                    tiles.append(halves[tile % len(halves)][part] * keep)
                ref[entry, begin : begin + 16, :] = jnp.concatenate(tiles, 0).astype(jnp.bfloat16)


def phase_tables(first_level, count, inner_bits, tile, angle, cos_ref, sin_ref):
    half = cos_ref.shape[0]
    bits = half.bit_length() - 1
    lane = iota((1, LANES), 1)
    step = jnp.ones((1, LANES), jnp.float32)
    mask = jnp.zeros((1, LANES), jnp.int32)
    tile_start = jnp.zeros((1, LANES), jnp.int32)
    for level in range(count):
        width = inner_bits + level
        here = (lane >> 2) == level
        step = jnp.where(here, 2.0 ** -(first_level + level), step)
        mask = jnp.where(here, 2**width - 1, mask)
        tile_start = jnp.where(here, tile * 2**width, tile_start)
    norm = 1.0 / math.sqrt(2.0)
    beam = tile_start + (bit_reversed(iota((8, LANES), 0), bits) & mask)
    j_index = (2 * beam + (lane & 1)).astype(jnp.float32)
    phi = angle * ((j_index + 0.5) * step - 1.0)
    inner = (jnp.cos(phi) * norm, jnp.sin(phi) * norm)
    groups = half // 8
    shape = (-(-groups // 8) * 8, LANES)
    beam = bit_reversed(iota(shape, 0) << 3, bits) & mask
    phi = angle * ((2 * beam).astype(jnp.float32) * step)
    outer = (jnp.cos(phi), jnp.sin(phi))
    for group in range(groups):
        co, si = cmul(inner, [part[group : group + 1, :] for part in outer])
        cos_ref[8 * group : 8 * group + 8, :] = co
        sin_ref[8 * group : 8 * group + 8, :] = si


def tables_kernel(total_freq, local, inner, fold, echo_hbm, matched_hbm, offsets_hbm, fraction_hbm,
                  tilt_hbm, order_hbm, echo_ref, order_ref, table_ref, high_ref, low_ref,
                  cos_ref, sin_ref, cos2_ref, sin2_ref, start_ref, edge_ref, band_ref, angle_ref,
                  matched_ref, offsets_ref, fraction_ref, tilt_ref, sems):
    pairs = (
        (matched_hbm, matched_ref),
        (offsets_hbm, offsets_ref),
        (fraction_hbm, fraction_ref),
        (tilt_hbm, tilt_ref),
        (order_hbm, order_ref),
        (echo_hbm, echo_ref),
    )
    copies = [pltpu.make_async_copy(*pair, sems.at[n]) for n, pair in enumerate(pairs)]
    for copy in copies:
        copy.start()
    tiles = echo_ref.shape[1]
    freq = tiles * LANES
    bands, apertures = lax.axis_size("band"), lax.axis_size("aperture")
    band = lax.axis_index("band")
    levels = start_ref.shape[0] // 4
    firsts = [(band ^ side) * freq for side in range(fold)]
    units = [unit_rows(total_freq, first, tiles) for first in firsts]
    copies[0].wait()
    for side in range(fold):
        make_table(total_freq, firsts[side], units[side], matched_ref, table_ref, side * tiles)
    for copy in copies[1:4]:
        copy.wait()
    build_starts(levels, offsets_ref, fraction_ref, start_ref, edge_ref)
    angle_ref[0:1, :] = build_angles(0, local, tilt_ref)
    angle_ref[1:2, :] = build_angles(local, levels - local, tilt_ref)
    build_matrices(start_ref, edge_ref, band_ref, high_ref, low_ref)
    phase_tables(0, local, 0, 0, angle_ref[0:1, :], cos_ref, sin_ref)
    place = lax.axis_index("aperture") * bands + band
    tile = bit_reversed(place, (bands * apertures).bit_length() - 1)
    phase_tables(local, levels - local, inner, tile, angle_ref[1:2, :], cos2_ref, sin2_ref)
    for copy in copies[4:]:
        copy.wait()


def interpolated(held, at, high_ref, low_ref):
    high, low = halves_of(held)
    m_high, m_low = (
        jnp.concatenate([ref[at], ref[at + 1]], axis=1) for ref in (high_ref, low_ref)
    )
    dot = functools.partial(jnp.dot, preferred_element_type=jnp.float32)
    rows = held.shape[0]
    if 4 * rows <= R:
        stacked = dot(jnp.concatenate([high, low], axis=0), m_high)
        return (stacked[:rows] + stacked[rows:]) + dot(high, m_low)
    left = jnp.concatenate([high, low, high], axis=1)
    return dot(left, jnp.concatenate([m_high, m_high, m_low], axis=0))


def children_of(source, half):
    return [source[pl.ds(child, 2 * half, stride=2), :] for child in range(2)]


def level_step(level, half, children, tables, high_ref, low_ref):
    cos_ref, sin_ref = tables
    products = [
        interpolated(held, 4 * level + 2 * child, high_ref, low_ref)
        for child, held in enumerate(children)
    ]
    result = []
    for parity in range(2):
        re = im = None
        for child in range(2):
            entry = 4 * level + 2 * child + parity
            co = cos_ref[:, entry : entry + 1]
            si = sin_ref[:, entry : entry + 1]
            p_re = products[child][0:half, parity * R : (parity + 1) * R]
            p_im = products[child][half:, parity * R : (parity + 1) * R]
            r_new = p_re * co - p_im * si
            i_new = p_re * si + p_im * co
            re = r_new if re is None else re + r_new
            im = i_new if im is None else im + i_new
        result.append((re, im))
    return result


def product_kernel(fold, *refs):
    bands = lax.axis_size("band")
    echoes, refs = refs[:fold], refs[fold:]
    table_ref, high_ref, low_ref, cos_ref, sin_ref, prof_ref, sum_ref = refs
    pulses, tiles = echoes[0].shape[:2]
    group = pulses // bands
    held = bands // fold
    core = lax.axis_index("band") & (fold - 1)
    pieces = []
    for echo_ref in echoes:
        for n in range(tiles):
            members = [
                echo_ref[pl.ds((member * fold + core) * group, group), n].reshape(2 * group, LANES)
                for member in range(held)
            ]
            pieces.append(jnp.concatenate(members, axis=0))
    table = jnp.concatenate([table_ref[n] for n in range(fold * tiles)], axis=1)
    sums = lax.dot_general(
        jnp.concatenate(pieces, axis=1),
        table,
        (((1,), (1,)), ((), ())),
        preferred_element_type=jnp.float32,
    )
    sum_ref[0] = sums[:, 0:R]
    sum_ref[1] = sums[:, R:]
    rows = group * held
    even, odd = pl.ds(0, rows, stride=2), pl.ds(1, rows, stride=2)
    values = (sum_ref[0, even, :] - sum_ref[1, odd, :], sum_ref[1, even, :] + sum_ref[0, odd, :])
    both = jnp.concatenate(values, axis=0)
    for child in range(2):
        result = interpolated(both, 2 * child, high_ref, low_ref)
        for parity in range(2):
            entry = 2 * child + parity
            phase = (cos_ref[0:1, entry : entry + 1], sin_ref[0:1, entry : entry + 1])
            column = slice(parity * R, (parity + 1) * R)
            turned = cmul((result[0:rows, column], result[rows:, column]), phase)
            for part, value in enumerate(turned):
                for side, half in enumerate(halves_of(value)):
                    at = (2 * side + child) * group
                    for member in range(held):
                        prof_ref[parity, part, member, at : at + group, :] = half[
                            member * group : (member + 1) * group
                        ]


def local_kernel(count, fold, *refs):
    bands = lax.axis_size("band")
    devices = bands * lax.axis_size("aperture")
    held = bands // fold
    orders, refs = refs[:held], refs[held:]
    prof_ref, high_ref, low_ref, cos_ref, sin_ref, out_ref, image_ref, pick_ref = refs
    group = prof_ref.shape[3] // 4
    rows = group * held
    half = rows // 2
    me = lax.axis_index("band") // fold
    for apart in range(held):
        member = me ^ apart
        start = pl.multiple_of(member * group, group)
        match = iota((group, group), 0) == jnp.broadcast_to(orders[apart][...], (group, group))
        lane = iota((group, group), 1)
        chosen = [jnp.where(match & (lane & 1 == child), 1.0, 0.0) for child in range(2)]
        chosen = jnp.concatenate(chosen + chosen, axis=0).astype(jnp.bfloat16)
        for parity in range(2):
            moved = lax.dot_general(
                chosen,
                jnp.concatenate([prof_ref[parity, part, member] for part in range(2)], axis=1),
                (((0,), (0,)), ((), ())),
                preferred_element_type=jnp.float32,
            )
            for part in range(2):
                pick_ref[parity, part, pl.ds(start, group), :] = moved[:, part * R : (part + 1) * R]
    for level in range(1, count):
        source, target = image_ref.at[level % 2], image_ref.at[(level + 1) % 2]
        if level == 1:
            children = []
            for child in range(0, 4, 2):
                parts = [
                    pick_ref[parity, part, pl.ds(child, rows // 4, stride=4), :]
                    + pick_ref[parity, part, pl.ds(child + 1, rows // 4, stride=4), :]
                    for part in range(2)
                    for parity in range(2)
                ]
                children.append(jnp.concatenate(parts, axis=0))
        else:
            children = children_of(source, half)
        result = level_step(level, half, children, (cos_ref, sin_ref), high_ref, low_ref)
        for parity in range(2):
            for part in range(2):
                target[pl.ds(part * rows + parity * half, half), :] = result[parity][part]
    last = image_ref.at[count % 2]
    per = rows // devices
    for part in range(2):
        for unit in range(per):
            if fold == 1:
                value = last[pl.ds(part * rows + unit * devices, devices), :]
            else:
                value = last[pl.ds(part * rows + unit, devices, stride=per), :]
            out_ref[pl.ds(part * per + unit, devices, stride=2 * per), :] = value


def box(rows):
    total = rows[0]
    for row in rows[1:]:
        total = total + row
    lane = iota(total.shape, 1)
    summed = total
    for off in (1, 2):
        right = pltpu.roll(total, off, 1)
        left = pltpu.roll(total, LANES - off, 1)
        summed = summed + jnp.where(lane >= off, right, 0.0)
        summed = summed + jnp.where(lane < LANES - off, left, 0.0)
    return summed


def near_count(position, size):
    return jnp.minimum(position, 2) + jnp.minimum(size - 1 - position, 2) + 1


def final_kernel(first_level, count, fold, recv_ref, high_ref, low_ref, cos_ref, sin_ref, out_ref,
                 image_ref, pad_ref):
    bands, apertures = lax.axis_size("band"), lax.axis_size("aperture")
    rows = out_ref.shape[0]
    half = rows // 2
    per = recv_ref.shape[0] // (2 * bands * apertures)
    high_ref = high_ref.at[4 * first_level : 4 * (first_level + count)]
    low_ref = low_ref.at[4 * first_level : 4 * (first_level + count)]
    for part in range(2):
        for unit in range(per):
            for core in range(fold):
                total = None
                for band in range(core, bands, fold):
                    begin = (band * 2 + part) * per + unit
                    value = recv_ref[pl.ds(begin, apertures, stride=bands * 2 * per), :]
                    total = value if total is None else total + value
                if fold == 1:
                    place = pl.ds(part * rows + unit * apertures, apertures)
                else:
                    place = pl.ds(part * rows + unit * fold + core, apertures, stride=bands)
                image_ref[0, place, :] = total
    for level in range(count):
        source, target = image_ref.at[level % 2], image_ref.at[(level + 1) % 2]
        children = children_of(source, half)
        result = level_step(level, half, children, (cos_ref, sin_ref), high_ref, low_ref)
        for parity in range(2):
            for part in range(2):
                target[pl.ds(part * rows + parity * half, half), :] = result[parity][part]
    last = image_ref.at[count % 2]
    power = last[0:rows, :] ** 2 + last[rows : 2 * rows, :] ** 2
    image_ref[(count + 1) % 2, 0:rows, :] = power
    edge = 8
    for part in range(2):
        pad_ref[part, 0:edge, :] = jnp.zeros((edge, LANES), jnp.float32)
        pad_ref[part, edge + rows :, :] = jnp.zeros((edge, LANES), jnp.float32)
    bits = rows.bit_length() - 1
    for row in range(rows):
        from_row = bit_reversed(row, bits)
        pad_ref[0, edge + row : edge + row + 1, :] = image_ref[
            (count + 1) % 2, from_row : from_row + 1, :
        ]
    power = pad_ref[0, edge : edge + rows, :]
    pad_ref[1, edge : edge + rows, :] = power * power
    sums = [
        box([pad_ref[part, edge + off : edge + off + rows, :] for off in range(-2, 3)])
        for part in range(2)
    ]
    shape = (rows, LANES)
    cells = near_count(iota(shape, 0), rows) * near_count(iota(shape, 1), LANES)
    cells = cells.astype(jnp.float32)
    mean, square = sums[0] / cells, sums[1] / cells
    gain = (square - mean * mean) / (square - 0.75 * mean * mean + 0.001)
    out_ref[...] = mean + gain * (power - mean)


def body(raw_echoes, pulse_order, matched, offsets, fraction, tilt_angle):
    bands, apertures = lax.axis_size("band"), lax.axis_size("aperture")
    devices = bands * apertures
    pulses, _, freq = raw_echoes.shape
    group = pulse_order.shape[-1]
    levels = tilt_angle.shape[0]
    tiles = freq // LANES
    fold = 2 if group == devices and bands % 2 == 0 else 1
    held = bands // fold
    rows = group * held
    local = (rows if fold == 1 else group).bit_length() - 1
    rest = levels - local
    inner = local - (devices.bit_length() - 1)
    per = rows // devices
    f32, bf16 = jnp.float32, jnp.bfloat16
    shape_of = jax.ShapeDtypeStruct
    vmem = pl.BlockSpec(memory_space=VMEM)
    params = pltpu.CompilerParams(vmem_limit_bytes=16 * 2**20)
    order = pulse_order.reshape(1, group)
    orders = [order]
    for apart in range(fold, bands, fold):
        orders.append(lax.ppermute(order, "band", [(n, n ^ apart) for n in range(bands)]))
    echo_parts = [raw_echoes]
    for side in range(1, fold):
        pairs = [(n, n ^ side) for n in range(bands)]
        echo_parts.append(lax.ppermute(raw_echoes, "band", pairs))
    echoes = [
        part.reshape(pulses, 2, tiles, LANES).transpose(0, 2, 1, 3) for part in echo_parts
    ]
    views = (
        echoes[0],
        matched,
        offsets.transpose(1, 2, 3, 0),
        fraction.transpose(1, 2, 0),
        tilt_angle.transpose(1, 0),
        order,
    )
    views = [pltpu.with_memory_space_constraint(view, pltpu.HBM) for view in views]
    tables = pl.pallas_call(
        functools.partial(tables_kernel, matched.shape[1], local, inner, fold),
        out_shape=[
            shape_of(echoes[0].shape, bf16),
            shape_of(order.shape, order.dtype),
            shape_of((fold * tiles, 2 * R, LANES), bf16),
            shape_of((4 * levels, R, R), bf16),
            shape_of((4 * levels, R, R), bf16),
            shape_of((rows // 2, LANES), f32),
            shape_of((rows // 2, LANES), f32),
            shape_of((group // 2, LANES), f32),
            shape_of((group // 2, LANES), f32),
        ],
        in_specs=[pl.BlockSpec(memory_space=pltpu.HBM)] * 6,
        out_specs=[vmem] * 9,
        scratch_shapes=[
            VMEM((4 * levels, 8, LANES), f32),
            VMEM((2, 4 * levels, 8, LANES), f32),
            VMEM((R // 8, 8, LANES), f32),
            VMEM((8, LANES), f32),
            VMEM(matched.shape, f32),
            SMEM(views[2].shape, jnp.int32),
            SMEM(views[3].shape, f32),
            SMEM(views[4].shape, f32),
            pltpu.SemaphoreType.DMA((6,)),
        ],
        cost_estimate=pl.CostEstimate(
            flops=400 * levels * R * R, bytes_accessed=16 * levels * R * R, transcendentals=0
        ),
        compiler_params=params,
        name="tables",
    )
    echoes[0], orders[0], table, high, low, cos_1, sin_1, cos_2, sin_2 = tables(*views)
    product = pl.pallas_call(
        functools.partial(product_kernel, fold),
        out_shape=shape_of((2, 2, held, 4 * group, R), bf16),
        in_specs=[vmem] * (fold + 5),
        out_specs=vmem,
        scratch_shapes=[VMEM((2, 2 * rows, R), f32)],
        cost_estimate=pl.CostEstimate(
            flops=8 * pulses * freq * R, bytes_accessed=4 * pulses * freq, transcendentals=0
        ),
        compiler_params=params,
        name="product",
    )
    prof = product(*echoes, table, high, low, cos_1, sin_1)
    sent = pl.pallas_call(
        functools.partial(local_kernel, local, fold),
        out_shape=shape_of((devices * 2 * per, R), f32),
        in_specs=[vmem] * (held + 5),
        out_specs=vmem,
        scratch_shapes=[VMEM((2, 2 * rows, R), f32), VMEM((2, 2, rows, R), f32)],
        compiler_params=params,
        name="levels",
    )(*orders, prof, high, low, cos_1, sin_1)
    received = lax.all_to_all(
        sent.reshape(devices, 2 * per, R), ("aperture", "band"), 0, 0, tiled=True
    ).reshape(devices * 2 * per, R)
    return pl.pallas_call(
        functools.partial(final_kernel, local, rest, fold),
        out_shape=shape_of((group, R), f32),
        in_specs=[vmem] * 5,
        out_specs=vmem,
        scratch_shapes=[VMEM((2, 2 * group, R), f32), VMEM((2, group + 16, R), f32)],
        compiler_params=params,
        name="finish",
    )(received, high, low, cos_2, sin_2)


def solution(mesh):
    in_specs = (P("aperture", None, "band"), P("aperture", "band", None), P(), P(), P(), P())
    out_specs = P(("band", "aperture"), None)

    return jax.shard_map(body, mesh=mesh, in_specs=in_specs, out_specs=out_specs, check_vma=False)
```

```python
import functools
import math

import jax
import jax.numpy as jnp
from jax import lax
from jax.experimental import pallas as pl
from jax.experimental.pallas import tpu as pltpu
from jax.sharding import PartitionSpec as P

R = 128
SHIFT = 8
LANES = 128
VMEM = pltpu.VMEM
SMEM = pltpu.SMEM


def iota(shape, axis):
    return lax.broadcasted_iota(jnp.int32, shape, axis)


def bit_reversed(value, bits):
    result = value & 0
    for bit in range(bits):
        result = result | (((value >> bit) & 1) << (bits - 1 - bit))
    return result


def halves_of(value):
    high = value.astype(jnp.bfloat16)
    low = (value - high.astype(jnp.float32)).astype(jnp.bfloat16)
    return high, low


def cmul(first, second):
    return (
        first[0] * second[0] - first[1] * second[1],
        first[0] * second[1] + first[1] * second[0],
    )


def unit_rows(total_freq, start, chunks):
    turn = 2.0 * math.pi / total_freq
    rows = -(-chunks // 8) * 8
    f_index = start + iota((rows, LANES), 0) * LANES + iota((rows, LANES), 1)
    angle = f_index.astype(jnp.float32) * turn
    rows = (jnp.cos(angle), jnp.sin(angle))
    sub = iota((8, LANES), 0)
    result = []
    for chunk in range(chunks):
        power = [jnp.broadcast_to(part[chunk : chunk + 1, :], (8, LANES)) for part in rows]
        low = None
        for bit in range(3):
            chosen = (sub >> bit) & 1 == 1
            factor = (jnp.where(chosen, power[0], 1.0), jnp.where(chosen, power[1], 0.0))
            low = factor if low is None else cmul(low, factor)
            power = cmul(power, power)
        result.append((low, power))
    return result


def make_table(total_freq, start, units, matched_ref, table_ref, first):
    scale = 1.0 / math.sqrt(total_freq)
    for chunk, (low, power) in enumerate(units):
        lanes = pl.ds(pl.multiple_of(start + chunk * LANES, LANES), LANES)
        spec = matched_ref[:, lanes] * scale
        low = cmul([jnp.broadcast_to(spec[n : n + 1, :], (8, LANES)) for n in range(2)], low)
        block = [jnp.concatenate(parts, axis=0) for parts in zip(low, cmul(low, power))]
        power = cmul(power, power)
        power = [jnp.concatenate([part, part], axis=0) for part in power]
        for begin in range(0, R, 16):
            table_ref[first + chunk, begin : begin + 16, :] = block[0].astype(jnp.bfloat16)
            table_ref[first + chunk, R + begin : R + begin + 16, :] = block[1].astype(jnp.bfloat16)
            if begin + 16 < R:
                block = cmul(block, power)


def edge_bands():
    lane = iota((8, LANES), 1)
    period = 4 * SHIFT
    result = []
    for begin in range(0, R, 8):
        first = begin - SHIFT - 4
        result.append(jnp.where((lane >= first) & (lane < first + period), 1.0, 0.0))
    return result


def build_starts(levels, offsets_ref, fraction_ref, start_ref):
    period = 4 * SHIFT
    lane, row = iota((8, LANES), 1), iota((8, LANES), 0)
    near_tap = lane & (period - 1)
    tap = jnp.where(near_tap < period // 2, -near_tap, period - near_tap).astype(jnp.float32)
    entries = [(n, c, p) for n in range(levels) for c in range(2) for p in range(2)]
    for block in range(0, len(entries), 8):
        here = entries[block : block + 8]
        shift = jnp.zeros((8, LANES), jnp.float32)
        for sub, (level, child, parity) in enumerate(here):
            shift = jnp.where(row == sub, fraction_ref[child, parity, level], shift)
        dist = tap - shift
        turn = math.pi * dist
        near = jnp.abs(dist) < 1e-12
        sinc = jnp.where(near, 1.0, jnp.sin(turn) / jnp.where(near, 1.0, turn))
        taper = sinc * jnp.exp(-((dist / 2.5) ** 2))
        taper = jnp.where(jnp.abs(dist) <= 4.0, taper, 0.0)
        for sub, (level, child, parity) in enumerate(here):
            moved = offsets_ref[child, parity, 0, level] - SHIFT
            one = jnp.broadcast_to(taper[sub : sub + 1, :], (8, LANES))
            one = pltpu.roll(one, (LANES - moved) & (LANES - 1), 1)
            start_ref[block + sub] = pltpu.roll(one, 0, 1, stride=1, stride_axis=0)


def build_angles(first_level, count, tilt_ref):
    lane = iota((1, LANES), 1)
    angle = jnp.zeros((1, LANES), jnp.float32)
    for level in range(count):
        for child in range(2):
            angle = jnp.where(
                (lane >> 1) == 2 * level + child, tilt_ref[child, first_level + level], angle
            )
    return angle


def build_matrices(offsets_ref, start_ref, band_ref, high_ref, low_ref):
    period = 4 * SHIFT
    for tile, band in enumerate(edge_bands()):
        band_ref[tile] = band
    last = R // 8 - 1
    row = iota((8, LANES), 0)
    for entry in range(start_ref.shape[0]):
        one = start_ref[entry]
        moved = offsets_ref[entry // 2 % 2, entry % 2, 0, entry // 4] - SHIFT
        edges = {
            0: jnp.where(row >= moved, band_ref[0], 0.0),
            last: jnp.where(row < moved + 8, band_ref[last], 0.0),
        }
        turned = [one] + [pltpu.roll(one, begin, 1) for begin in range(8, period, 8)]
        halves = []
        for value in turned:
            high = value.astype(jnp.bfloat16).astype(jnp.float32)
            halves.append((high, value - high))
        for begin in range(0, R, 16):
            for part, ref in enumerate((high_ref, low_ref)):
                tiles = []
                for tile in (begin // 8, begin // 8 + 1):
                    keep = edges[tile] if tile in edges else band_ref[tile]
                    tiles.append(halves[tile % len(halves)][part] * keep)
                ref[entry, begin : begin + 16, :] = jnp.concatenate(tiles, 0).astype(jnp.bfloat16)


def phase_tables(first_level, count, inner_bits, tile, angle, cos_ref, sin_ref):
    half = cos_ref.shape[0]
    bits = half.bit_length() - 1
    lane = iota((1, LANES), 1)
    step = jnp.ones((1, LANES), jnp.float32)
    mask = jnp.zeros((1, LANES), jnp.int32)
    tile_start = jnp.zeros((1, LANES), jnp.int32)
    for level in range(count):
        width = inner_bits + level
        here = (lane >> 2) == level
        step = jnp.where(here, 2.0 ** -(first_level + level), step)
        mask = jnp.where(here, 2**width - 1, mask)
        tile_start = jnp.where(here, tile * 2**width, tile_start)
    norm = 1.0 / math.sqrt(2.0)
    beam = tile_start + (bit_reversed(iota((8, LANES), 0), bits) & mask)
    j_index = (2 * beam + (lane & 1)).astype(jnp.float32)
    phi = angle * ((j_index + 0.5) * step - 1.0)
    inner = (jnp.cos(phi) * norm, jnp.sin(phi) * norm)
    groups = half // 8
    shape = (-(-groups // 8) * 8, LANES)
    beam = bit_reversed(iota(shape, 0) << 3, bits) & mask
    phi = angle * ((2 * beam).astype(jnp.float32) * step)
    outer = (jnp.cos(phi), jnp.sin(phi))
    for group in range(groups):
        co, si = cmul(inner, [part[group : group + 1, :] for part in outer])
        cos_ref[8 * group : 8 * group + 8, :] = co
        sin_ref[8 * group : 8 * group + 8, :] = si


def tables_kernel(total_freq, local, inner, fold, echo_hbm, matched_hbm, offsets_hbm, fraction_hbm,
                  tilt_hbm, order_hbm, echo_ref, order_ref, table_ref, high_ref, low_ref,
                  cos_ref, sin_ref, cos2_ref, sin2_ref, start_ref, band_ref, angle_ref,
                  matched_ref, offsets_ref, fraction_ref, tilt_ref, sems):
    pairs = (
        (matched_hbm, matched_ref),
        (offsets_hbm, offsets_ref),
        (fraction_hbm, fraction_ref),
        (tilt_hbm, tilt_ref),
        (order_hbm, order_ref),
        (echo_hbm, echo_ref),
    )
    copies = [pltpu.make_async_copy(*pair, sems.at[n]) for n, pair in enumerate(pairs)]
    for copy in copies:
        copy.start()
    tiles = echo_ref.shape[1]
    freq = tiles * LANES
    bands, apertures = lax.axis_size("band"), lax.axis_size("aperture")
    band = lax.axis_index("band")
    levels = start_ref.shape[0] // 4
    firsts = [(band ^ side) * freq for side in range(fold)]
    units = [unit_rows(total_freq, first, tiles) for first in firsts]
    copies[0].wait()
    for side in range(fold):
        make_table(total_freq, firsts[side], units[side], matched_ref, table_ref, side * tiles)
    for copy in copies[1:4]:
        copy.wait()
    build_starts(levels, offsets_ref, fraction_ref, start_ref)
    angle_ref[0:1, :] = build_angles(0, local, tilt_ref)
    angle_ref[1:2, :] = build_angles(local, levels - local, tilt_ref)
    build_matrices(offsets_ref, start_ref, band_ref, high_ref, low_ref)
    phase_tables(0, local, 0, 0, angle_ref[0:1, :], cos_ref, sin_ref)
    place = lax.axis_index("aperture") * bands + band
    tile = bit_reversed(place, (bands * apertures).bit_length() - 1)
    phase_tables(local, levels - local, inner, tile, angle_ref[1:2, :], cos2_ref, sin2_ref)
    for copy in copies[4:]:
        copy.wait()


def interpolated(held, at, high_ref, low_ref):
    high, low = halves_of(held)
    m_high, m_low = (
        jnp.concatenate([ref[at], ref[at + 1]], axis=1) for ref in (high_ref, low_ref)
    )
    dot = functools.partial(jnp.dot, preferred_element_type=jnp.float32)
    rows = held.shape[0]
    if 4 * rows <= R:
        stacked = dot(jnp.concatenate([high, low], axis=0), m_high)
        return (stacked[:rows] + stacked[rows:]) + dot(high, m_low)
    left = jnp.concatenate([high, low, high], axis=1)
    return dot(left, jnp.concatenate([m_high, m_high, m_low], axis=0))


def children_of(source, half):
    return [source[pl.ds(child, 2 * half, stride=2), :] for child in range(2)]


def level_step(level, half, children, tables, high_ref, low_ref):
    cos_ref, sin_ref = tables
    products = [
        interpolated(held, 4 * level + 2 * child, high_ref, low_ref)
        for child, held in enumerate(children)
    ]
    result = []
    for parity in range(2):
        re = im = None
        for child in range(2):
            entry = 4 * level + 2 * child + parity
            co = cos_ref[:, entry : entry + 1]
            si = sin_ref[:, entry : entry + 1]
            p_re = products[child][0:half, parity * R : (parity + 1) * R]
            p_im = products[child][half:, parity * R : (parity + 1) * R]
            r_new = p_re * co - p_im * si
            i_new = p_re * si + p_im * co
            re = r_new if re is None else re + r_new
            im = i_new if im is None else im + i_new
        result.append((re, im))
    return result


def product_kernel(fold, *refs):
    bands = lax.axis_size("band")
    echoes, refs = refs[:fold], refs[fold:]
    table_ref, high_ref, low_ref, cos_ref, sin_ref, prof_ref, sum_ref = refs
    pulses, tiles = echoes[0].shape[:2]
    group = pulses // bands
    held = bands // fold
    core = lax.axis_index("band") & (fold - 1)
    pieces = []
    for echo_ref in echoes:
        for n in range(tiles):
            members = [
                echo_ref[pl.ds((member * fold + core) * group, group), n].reshape(2 * group, LANES)
                for member in range(held)
            ]
            pieces.append(jnp.concatenate(members, axis=0))
    table = jnp.concatenate([table_ref[n] for n in range(fold * tiles)], axis=1)
    sums = lax.dot_general(
        jnp.concatenate(pieces, axis=1),
        table,
        (((1,), (1,)), ((), ())),
        preferred_element_type=jnp.float32,
    )
    sum_ref[0] = sums[:, 0:R]
    sum_ref[1] = sums[:, R:]
    rows = group * held
    even, odd = pl.ds(0, rows, stride=2), pl.ds(1, rows, stride=2)
    values = (sum_ref[0, even, :] - sum_ref[1, odd, :], sum_ref[1, even, :] + sum_ref[0, odd, :])
    both = jnp.concatenate(values, axis=0)
    for child in range(2):
        result = interpolated(both, 2 * child, high_ref, low_ref)
        for parity in range(2):
            entry = 2 * child + parity
            phase = (cos_ref[0:1, entry : entry + 1], sin_ref[0:1, entry : entry + 1])
            column = slice(parity * R, (parity + 1) * R)
            turned = cmul((result[0:rows, column], result[rows:, column]), phase)
            for part, value in enumerate(turned):
                for side, half in enumerate(halves_of(value)):
                    at = (2 * side + child) * group
                    for member in range(held):
                        prof_ref[parity, part, member, at : at + group, :] = half[
                            member * group : (member + 1) * group
                        ]


def local_kernel(count, fold, *refs):
    bands = lax.axis_size("band")
    devices = bands * lax.axis_size("aperture")
    held = bands // fold
    orders, refs = refs[:held], refs[held:]
    prof_ref, high_ref, low_ref, cos_ref, sin_ref, out_ref, image_ref, pick_ref = refs
    group = prof_ref.shape[3] // 4
    rows = group * held
    half = rows // 2
    me = lax.axis_index("band") // fold
    for apart in range(held):
        member = me ^ apart
        start = pl.multiple_of(member * group, group)
        match = iota((group, group), 0) == jnp.broadcast_to(orders[apart][...], (group, group))
        lane = iota((group, group), 1)
        chosen = [jnp.where(match & (lane & 1 == child), 1.0, 0.0) for child in range(2)]
        chosen = jnp.concatenate(chosen + chosen, axis=0).astype(jnp.bfloat16)
        for parity in range(2):
            moved = lax.dot_general(
                chosen,
                jnp.concatenate([prof_ref[parity, part, member] for part in range(2)], axis=1),
                (((0,), (0,)), ((), ())),
                preferred_element_type=jnp.float32,
            )
            for part in range(2):
                pick_ref[parity, part, pl.ds(start, group), :] = moved[:, part * R : (part + 1) * R]
    for level in range(1, count):
        source, target = image_ref.at[level % 2], image_ref.at[(level + 1) % 2]
        if level == 1:
            children = []
            for child in range(0, 4, 2):
                parts = [
                    pick_ref[parity, part, pl.ds(child, rows // 4, stride=4), :]
                    + pick_ref[parity, part, pl.ds(child + 1, rows // 4, stride=4), :]
                    for part in range(2)
                    for parity in range(2)
                ]
                children.append(jnp.concatenate(parts, axis=0))
        else:
            children = children_of(source, half)
        result = level_step(level, half, children, (cos_ref, sin_ref), high_ref, low_ref)
        for parity in range(2):
            for part in range(2):
                target[pl.ds(part * rows + parity * half, half), :] = result[parity][part]
    last = image_ref.at[count % 2]
    per = rows // devices
    for part in range(2):
        for unit in range(per):
            if fold == 1:
                value = last[pl.ds(part * rows + unit * devices, devices), :]
            else:
                value = last[pl.ds(part * rows + unit, devices, stride=per), :]
            out_ref[pl.ds(part * per + unit, devices, stride=2 * per), :] = value


def box(rows):
    total = rows[0]
    for row in rows[1:]:
        total = total + row
    lane = iota(total.shape, 1)
    summed = total
    for off in (1, 2):
        right = pltpu.roll(total, off, 1)
        left = pltpu.roll(total, LANES - off, 1)
        summed = summed + jnp.where(lane >= off, right, 0.0)
        summed = summed + jnp.where(lane < LANES - off, left, 0.0)
    return summed


def near_count(position, size):
    return jnp.minimum(position, 2) + jnp.minimum(size - 1 - position, 2) + 1


def final_kernel(first_level, count, fold, recv_ref, high_ref, low_ref, cos_ref, sin_ref, out_ref,
                 image_ref, pad_ref):
    bands, apertures = lax.axis_size("band"), lax.axis_size("aperture")
    rows = out_ref.shape[0]
    half = rows // 2
    per = recv_ref.shape[0] // (2 * bands * apertures)
    high_ref = high_ref.at[4 * first_level : 4 * (first_level + count)]
    low_ref = low_ref.at[4 * first_level : 4 * (first_level + count)]
    for part in range(2):
        for unit in range(per):
            for core in range(fold):
                total = None
                for band in range(core, bands, fold):
                    begin = (band * 2 + part) * per + unit
                    value = recv_ref[pl.ds(begin, apertures, stride=bands * 2 * per), :]
                    total = value if total is None else total + value
                if fold == 1:
                    place = pl.ds(part * rows + unit * apertures, apertures)
                else:
                    place = pl.ds(part * rows + unit * fold + core, apertures, stride=bands)
                image_ref[0, place, :] = total
    for level in range(count):
        source, target = image_ref.at[level % 2], image_ref.at[(level + 1) % 2]
        children = children_of(source, half)
        result = level_step(level, half, children, (cos_ref, sin_ref), high_ref, low_ref)
        for parity in range(2):
            for part in range(2):
                target[pl.ds(part * rows + parity * half, half), :] = result[parity][part]
    last = image_ref.at[count % 2]
    power = last[0:rows, :] ** 2 + last[rows : 2 * rows, :] ** 2
    image_ref[(count + 1) % 2, 0:rows, :] = power
    edge = 8
    for part in range(2):
        pad_ref[part, 0:edge, :] = jnp.zeros((edge, LANES), jnp.float32)
        pad_ref[part, edge + rows :, :] = jnp.zeros((edge, LANES), jnp.float32)
    bits = rows.bit_length() - 1
    for row in range(rows):
        from_row = bit_reversed(row, bits)
        pad_ref[0, edge + row : edge + row + 1, :] = image_ref[
            (count + 1) % 2, from_row : from_row + 1, :
        ]
    power = pad_ref[0, edge : edge + rows, :]
    pad_ref[1, edge : edge + rows, :] = power * power
    sums = [
        box([pad_ref[part, edge + off : edge + off + rows, :] for off in range(-2, 3)])
        for part in range(2)
    ]
    shape = (rows, LANES)
    cells = near_count(iota(shape, 0), rows) * near_count(iota(shape, 1), LANES)
    cells = cells.astype(jnp.float32)
    mean, square = sums[0] / cells, sums[1] / cells
    gain = (square - mean * mean) / (square - 0.75 * mean * mean + 0.001)
    out_ref[...] = mean + gain * (power - mean)


def body(raw_echoes, pulse_order, matched, offsets, fraction, tilt_angle):
    bands, apertures = lax.axis_size("band"), lax.axis_size("aperture")
    devices = bands * apertures
    pulses, _, freq = raw_echoes.shape
    group = pulse_order.shape[-1]
    levels = tilt_angle.shape[0]
    tiles = freq // LANES
    fold = 2 if group == devices and bands % 2 == 0 else 1
    held = bands // fold
    rows = group * held
    local = (rows if fold == 1 else group).bit_length() - 1
    rest = levels - local
    inner = local - (devices.bit_length() - 1)
    per = rows // devices
    f32, bf16 = jnp.float32, jnp.bfloat16
    shape_of = jax.ShapeDtypeStruct
    vmem = pl.BlockSpec(memory_space=VMEM)
    params = pltpu.CompilerParams(vmem_limit_bytes=16 * 2**20)
    order = pulse_order.reshape(1, group)
    orders = [order]
    for apart in range(fold, bands, fold):
        orders.append(lax.ppermute(order, "band", [(n, n ^ apart) for n in range(bands)]))
    echo_parts = [raw_echoes]
    for side in range(1, fold):
        pairs = [(n, n ^ side) for n in range(bands)]
        echo_parts.append(lax.ppermute(raw_echoes, "band", pairs))
    echoes = [
        part.reshape(pulses, 2, tiles, LANES).transpose(0, 2, 1, 3) for part in echo_parts
    ]
    views = (
        echoes[0],
        matched,
        offsets.transpose(1, 2, 3, 0),
        fraction.transpose(1, 2, 0),
        tilt_angle.transpose(1, 0),
        order,
    )
    views = [pltpu.with_memory_space_constraint(view, pltpu.HBM) for view in views]
    tables = pl.pallas_call(
        functools.partial(tables_kernel, matched.shape[1], local, inner, fold),
        out_shape=[
            shape_of(echoes[0].shape, bf16),
            shape_of(order.shape, order.dtype),
            shape_of((fold * tiles, 2 * R, LANES), bf16),
            shape_of((4 * levels, R, R), bf16),
            shape_of((4 * levels, R, R), bf16),
            shape_of((rows // 2, LANES), f32),
            shape_of((rows // 2, LANES), f32),
            shape_of((group // 2, LANES), f32),
            shape_of((group // 2, LANES), f32),
        ],
        in_specs=[pl.BlockSpec(memory_space=pltpu.HBM)] * 6,
        out_specs=[vmem] * 9,
        scratch_shapes=[
            VMEM((4 * levels, 8, LANES), f32),
            VMEM((R // 8, 8, LANES), f32),
            VMEM((8, LANES), f32),
            VMEM(matched.shape, f32),
            SMEM(views[2].shape, jnp.int32),
            SMEM(views[3].shape, f32),
            SMEM(views[4].shape, f32),
            pltpu.SemaphoreType.DMA((6,)),
        ],
        cost_estimate=pl.CostEstimate(
            flops=400 * levels * R * R, bytes_accessed=16 * levels * R * R, transcendentals=0
        ),
        compiler_params=params,
        name="tables",
    )
    echoes[0], orders[0], table, high, low, cos_1, sin_1, cos_2, sin_2 = tables(*views)
    product = pl.pallas_call(
        functools.partial(product_kernel, fold),
        out_shape=shape_of((2, 2, held, 4 * group, R), bf16),
        in_specs=[vmem] * (fold + 5),
        out_specs=vmem,
        scratch_shapes=[VMEM((2, 2 * rows, R), f32)],
        cost_estimate=pl.CostEstimate(
            flops=8 * pulses * freq * R, bytes_accessed=4 * pulses * freq, transcendentals=0
        ),
        compiler_params=params,
        name="product",
    )
    prof = product(*echoes, table, high, low, cos_1, sin_1)
    sent = pl.pallas_call(
        functools.partial(local_kernel, local, fold),
        out_shape=shape_of((devices * 2 * per, R), f32),
        in_specs=[vmem] * (held + 5),
        out_specs=vmem,
        scratch_shapes=[VMEM((2, 2 * rows, R), f32), VMEM((2, 2, rows, R), f32)],
        compiler_params=params,
        name="levels",
    )(*orders, prof, high, low, cos_1, sin_1)
    received = lax.all_to_all(
        sent.reshape(devices, 2 * per, R), ("aperture", "band"), 0, 0, tiled=True
    ).reshape(devices * 2 * per, R)
    return pl.pallas_call(
        functools.partial(final_kernel, local, rest, fold),
        out_shape=shape_of((group, R), f32),
        in_specs=[vmem] * 5,
        out_specs=vmem,
        scratch_shapes=[VMEM((2, 2 * group, R), f32), VMEM((2, group + 16, R), f32)],
        compiler_params=params,
        name="finish",
    )(received, high, low, cos_2, sin_2)


def solution(mesh):
    in_specs = (P("aperture", None, "band"), P("aperture", "band", None), P(), P(), P(), P())
    out_specs = P(("band", "aperture"), None)

    return jax.shard_map(body, mesh=mesh, in_specs=in_specs, out_specs=out_specs, check_vma=False)
```
